512 devices in a mesh: grp: 8 (over y_hi, x), blk: 64 (over z, y_lo, core).
Axes of the slice: x: 4, y: 8 (y_hi: 2, y_lo: 4; y = y_hi * 4 + y_lo), z: 8, core: 2. Of those that a mesh axis runs over, the one named last changes fastest.
Arguments:
- vertex_embed: float32 [196608, 256], P(('grp', 'blk')), may hold values from -1.8 to 1.8
- context_embed: float32 [196608, 256], P(('grp', 'blk')), may hold values from -1.8 to 1.8
- counts: int32 [4, 196608, 384], P(None, ('grp', 'blk')), may hold values from 0 to 7
- negatives: int32 [4, 5, 196608], P(None, None, ('grp', 'blk')), may hold values from 0 to 383
- masks: int32 [4, 1536, 3], P(None, ('grp', 'blk')), may hold values 0 or 1
Outputs:
- vertex_final: float32 [196608, 256], P(('grp', 'blk'))
- context_final: float32 [196608, 256], P(('grp', 'blk'))
The draws below stay inside these ranges and needn't reach their ends.
All inputs are finite; a program needn't handle non-finite values. No bound on the sum of `masks` on one device may be relied on, other than what follows from the above.
Results may differ from the reference program's by a relative error of at most 0.0003.
Values sent between devices are 32-bit elements; how exact they have to be, the bound alone decides.
No kernel may reach another device: no remote copies, remote signals or barrier semaphores. Data moves between devices by JAX's collectives and lax.ppermute only.
A program may use at most 64 MiB of HBM per device.

```python
import math
import jax
import jax.numpy as jnp
from jax import lax

W = 256
ROWS = 384
TILE = 128
NEGS = 5
ROUNDS = 2
ROUND_PASSES = 2
PASSES = 4
TILES = 3
VERTS = 196608
N_GRP = 8
N_BLK = 64
DEVICES = 512


def plant(drawn, stream_key, least, largest):
    extent = drawn.shape
    spot = [jax.random.randint(jax.random.fold_in(stream_key, axis), (), 0, extent[axis]) for axis in range(len(extent))]
    drawn = drawn.at[tuple(spot)].set(least)
    longest = extent.index(max(extent))
    spot[longest] = (spot[longest] + 1) % extent[longest]
    return drawn.at[tuple(spot)].set(largest)


def steps_of(stream_key, extent, pieces, low, largest):
    def one(dim, blocks):
        steps = jax.random.uniform(jax.random.fold_in(jax.random.fold_in(stream_key, 6), dim), (blocks,), jnp.float32, low / len(pieces), largest / len(pieces))
        return jnp.repeat(jnp.exp(steps), extent[dim] // blocks).reshape((-1,) + (1,) * (len(extent) - dim - 1))

    factor_of = one(*pieces[0])
    for cut in pieces[1:]:
        factor_of = factor_of * one(*cut)
    return factor_of


def normal_values(key, extent, width, limit, shards=(), kind=jnp.bfloat16):
    factor_of = steps_of(key, extent, shards, -0.22, 0.18) if shards else 1.0
    array = jax.random.normal(key, extent, jnp.float32) * width * factor_of
    return jnp.minimum(jnp.maximum(array, -limit), limit).astype(kind)


def setup_inputs(seed: int = 0) -> dict:
    key_of = jax.random.split(jax.random.key(seed), 6)
    return {
        "vertex_embed": normal_values(key_of[0], (VERTS, W), 0.3, 1.8, ((0, 512),), jnp.float32),
        "context_embed": normal_values(key_of[1], (VERTS, W), 0.3, 1.8, ((0, 512),), jnp.float32),
        "counts": plant(jax.random.randint(key_of[2], (PASSES, VERTS, ROWS), 0, 8), jax.random.fold_in(key_of[2], 1), 0, 7).astype(jnp.int32),
        "negatives": plant(jax.random.randint(key_of[3], (PASSES, NEGS, VERTS), 0, ROWS), jax.random.fold_in(key_of[3], 1), 0, ROWS - 1).astype(jnp.int32),
        "masks": plant((jax.random.randint(key_of[4], (PASSES, DEVICES * TILES, TILES), 0, 4) < 3).astype(jnp.int32), jax.random.fold_in(key_of[4], 1), 0, 1),
    }


def reference(vertex_embed, context_embed, counts, negatives, masks):
    highest = lax.Precision.HIGHEST
    vert = vertex_embed.reshape(N_GRP, N_BLK, ROWS, W)
    ctx = context_embed.reshape(N_GRP, N_BLK, ROWS, W)
    cnt = counts.reshape(PASSES, N_GRP, N_BLK, ROWS, ROWS)
    neg = negatives.reshape(PASSES, NEGS, N_GRP, N_BLK, ROWS)
    msk = masks.reshape(PASSES, N_GRP, N_BLK, TILES, TILES)
    columns = jnp.arange(ROWS, dtype=jnp.int32)
    eta = 0.25 / math.sqrt(ROWS)
    for rnd in range(ROUNDS):
        if rnd > 0:
            vert = jnp.flip(vert.reshape(N_GRP // 2, 2, N_BLK, ROWS, W), axis=1).reshape(N_GRP, N_BLK, ROWS, W)
        for step in range(ROUND_PASSES):
            index = rnd * ROUND_PASSES + step
            scores = jnp.einsum('gbiw,gbjw->gbij', vert, ctx, precision=highest)
            sig = jax.nn.sigmoid(scores)
            negcount = jnp.zeros((N_GRP, N_BLK, ROWS, ROWS), jnp.float32)
            for sample in range(NEGS):
                negcount = negcount + (neg[index, sample][..., :, None] == columns).astype(jnp.float32)
            coef = cnt[index].astype(jnp.float32) * (1.0 - sig) - negcount * sig
            gate = msk[index].astype(jnp.float32)[:, :, :, None, :, None]
            coef = (coef.reshape(N_GRP, N_BLK, TILES, TILE, TILES, TILE) * gate).reshape(N_GRP, N_BLK, ROWS, ROWS)
            new_vert = vert + eta * jnp.einsum('gbij,gbjw->gbiw', coef, ctx, precision=highest)
            new_ctx = ctx + eta * jnp.einsum('gbij,gbiw->gbjw', coef, vert, precision=highest)
            vert = new_vert
            ctx = jnp.roll(new_ctx, 1, axis=1)
    return (vert.reshape(VERTS, W), ctx.reshape(VERTS, W))
```

```python
import functools
import math

import jax
import jax.numpy as jnp
from jax import lax
from jax.experimental import pallas as pl
from jax.experimental.pallas import tpu as pltpu
from jax.sharding import PartitionSpec as P


F32 = jnp.float32
BF16 = jnp.bfloat16
NT = (((1,), (1,)), ((), ()))
NN = (((1,), (0,)), ((), ()))


def halves(x):
    high = x.astype(BF16)
    return high, (x - high.astype(F32)).astype(BF16)


def product(a, b, dims):
    dot = functools.partial(lax.dot_general, dimension_numbers=dims, preferred_element_type=F32)
    return dot(a[0], b[0]) + (dot(a[0], b[1]) + dot(a[1], b[0]))


def tables(step, slot, counts, neg_ref, mask_ref, base_ref, slope_ref):
    rows = counts.shape[0]
    tiles = mask_ref.shape[0]
    tile = rows // tiles
    scale = 0.125 / math.sqrt(rows)
    neg = jnp.transpose(neg_ref[:, step].astype(F32)).astype(jnp.int32)
    for ti in range(tiles):
        here = slice(ti * tile, (ti + 1) * tile)
        picks = [jnp.broadcast_to(neg[here, k : k + 1], (tile, tile)) for k in range(neg.shape[1])]
        for tj in range(tiles):
            there = slice(tj * tile, (tj + 1) * tile)
            column = lax.broadcasted_iota(jnp.int32, (tile, tile), 1) + tj * tile
            negcount = sum((pick == column).astype(F32) for pick in picks)
            cnt = counts[here, there].astype(F32)
            gate = mask_ref[ti, step, tj].astype(F32) * scale
            base_ref[slot, here, there] = (cnt - negcount) * gate
            slope_ref[slot, here, there] = (cnt + negcount) * gate


def pass_body(vert, ctx, base, slope):
    vs, cs = halves(vert), halves(ctx)
    coef = base - slope * jnp.tanh(0.5 * product(vs, cs, NT))
    new_ctx = ctx + product(halves(jnp.transpose(coef)), vs, NN)
    new_vert = vert + product(halves(coef), cs, NN)
    return new_vert, new_ctx


def first_kernel(vert_hbm, ctx_hbm, counts_hbm, neg_ref, mask_ref, new_vert_ref, new_ctx_ref, vert, ctx, cnt, base, slope, sems):
    copies = [
        pltpu.make_async_copy(counts_hbm.at[0], cnt, sems.at[0]),
        pltpu.make_async_copy(vert_hbm, vert, sems.at[1]),
        pltpu.make_async_copy(ctx_hbm, ctx, sems.at[2]),
    ]
    for copy in copies:
        copy.start()
    copies[0].wait()
    tables(0, 0, cnt, neg_ref, mask_ref, base, slope)
    copies[1].wait()
    copies[2].wait()
    new_vert_ref[...], new_ctx_ref[...] = pass_body(vert[...], ctx[...], base[0], slope[0])


def rest_kernel(after, counts_hbm, neg_ref, mask_ref, base_ref, slope_ref, cnt, sems):
    copies = [pltpu.make_async_copy(counts_hbm.at[i + 1], cnt.at[i], sems.at[i]) for i in range(cnt.shape[0])]
    for copy in copies:
        copy.start()
    for i, copy in enumerate(copies):
        copy.wait()
        tables(i + 1, i, cnt.at[i], neg_ref, mask_ref, base_ref, slope_ref)


def pass_kernel(step, core, after, vert_ref, ctx_ref, base_ref, slope_ref, new_vert_ref, new_ctx_ref):
    @pl.when(lax.axis_index("blk") % 2 == core)
    def _():
        new_vert_ref[...], new_ctx_ref[...] = pass_body(vert_ref[...], ctx_ref[...], base_ref[step - 1], slope_ref[step - 1])


def in_vmem(x):
    return pltpu.with_memory_space_constraint(x, pltpu.VMEM)


def in_hbm(x):
    return pltpu.with_memory_space_constraint(x, pltpu.HBM)


VMEM_SPEC = pl.BlockSpec(memory_space=pltpu.VMEM)
SMEM_SPEC = pl.BlockSpec(memory_space=pltpu.SMEM)
HBM_SPEC = pl.BlockSpec(memory_space=pltpu.HBM)
ANY_SPEC = pl.BlockSpec(memory_space=pl.ANY)


def params(mib):
    return pltpu.CompilerParams(vmem_limit_bytes=mib << 20)


def on_device(vertex_embed, context_embed, counts, negatives, masks):
    part = vertex_embed.shape
    passes, rows = counts.shape[0], counts.shape[1]
    negatives = jnp.transpose(negatives, (1, 0, 2))
    masks = jnp.transpose(masks, (1, 0, 2))
    state = pltpu.VMEM(part, F32)
    table = pltpu.VMEM((passes - 1, rows, rows), F32)
    square = pltpu.VMEM((1, rows, rows), F32)
    vert, out = pl.pallas_call(
        first_kernel,
        out_shape=(state, state),
        in_specs=[HBM_SPEC] * 3 + [VMEM_SPEC, SMEM_SPEC],
        out_specs=(VMEM_SPEC,) * 2,
        scratch_shapes=[state, state, pltpu.VMEM((rows, rows), jnp.int32), square, square, pltpu.SemaphoreType.DMA((3,))],
        compiler_params=params(20),
        name="first",
    )(in_hbm(vertex_embed), in_hbm(context_embed), in_hbm(counts), negatives, masks)
    base, slope = pl.pallas_call(
        rest_kernel,
        out_shape=(table, table),
        in_specs=[ANY_SPEC, HBM_SPEC, VMEM_SPEC, SMEM_SPEC],
        out_specs=(VMEM_SPEC,) * 2,
        scratch_shapes=[pltpu.VMEM((passes - 1, rows, rows), jnp.int32), pltpu.SemaphoreType.DMA((passes - 1,))],
        compiler_params=params(20),
        name="rest",
    )(vert, in_hbm(counts), negatives, masks)

    def one_pass(step, core, after, vert, ctx):
        return pl.pallas_call(
            functools.partial(pass_kernel, step, core),
            out_shape=(state, state),
            in_specs=[ANY_SPEC] + [VMEM_SPEC] * 4,
            out_specs=(VMEM_SPEC,) * 2,
            compiler_params=params(20),
        )(after, in_vmem(vert), in_vmem(ctx), in_vmem(base), in_vmem(slope))

    n_grp, n_blk = lax.axis_size("grp"), lax.axis_size("blk")

    def within_chip(value):
        return lax.ppermute(value, "blk", [(b, b + 1) for b in range(0, n_blk, 2)])

    def between_chips(value):
        return lax.ppermute(value, "blk", [(b, (b + 1) % n_blk) for b in range(1, n_blk, 2)])

    def swapped(core, value):
        pairs = [(g * n_blk + b, (g ^ 1) * n_blk + b) for g in range(n_grp) for b in range(core, n_blk, 2)]
        return lax.ppermute(value, ("grp", "blk"), pairs)

    x0 = between_chips(out)
    on0 = within_chip(out)
    vert_a, out_a = one_pass(1, 1, vert, vert, on0)
    x1 = between_chips(out_a)
    moved_a = swapped(1, vert_a)
    vert_b, out_b = one_pass(1, 0, vert_a, vert, x0)
    moved_b = swapped(0, vert_b)
    on1 = within_chip(out_b)
    vert_a, out_a = one_pass(2, 1, vert_b, moved_a, on1)
    x2 = between_chips(out_a)
    vert_b, out_b = one_pass(2, 0, vert_a, moved_b, x1)
    on2 = within_chip(out_b)
    vert_a, out_a = one_pass(3, 1, vert_b, vert_a, on2)
    x3 = between_chips(out_a)
    vert_b, out_b = one_pass(3, 0, vert_a, vert_b, x2)
    on3 = within_chip(out_b)
    odd = lax.axis_index("blk") % 2 == 1
    return jnp.where(odd, vert_a, vert_b), jnp.where(odd, on3, x3)


def solution(mesh):
    placed = (
        P(("grp", "blk"), None),
        P(("grp", "blk"), None),
        P(None, ("grp", "blk"), None),
        P(None, None, ("grp", "blk")),
        P(None, ("grp", "blk"), None),
    )

    return jax.shard_map(
        on_device,
        mesh=mesh,
        in_specs=placed,
        out_specs=(P(("grp", "blk"), None), P(("grp", "blk"), None)),
        check_vma=False,
    )
```

```python
import functools
import math

import jax
import jax.numpy as jnp
from jax import lax
from jax.experimental import pallas as pl
from jax.experimental.pallas import tpu as pltpu
from jax.sharding import PartitionSpec as P


F32 = jnp.float32
BF16 = jnp.bfloat16
NT = (((1,), (1,)), ((), ()))
NN = (((1,), (0,)), ((), ()))
CHUNK = 32

VMEM_SPEC = pl.BlockSpec(memory_space=pltpu.VMEM)
HBM_SPEC = pl.BlockSpec(memory_space=pltpu.HBM)
ANY_SPEC = pl.BlockSpec(memory_space=pl.ANY)


def in_vmem(x):
    return pltpu.with_memory_space_constraint(x, pltpu.VMEM)


def in_hbm(x):
    return pltpu.with_memory_space_constraint(x, pltpu.HBM)


def params(mib):
    return pltpu.CompilerParams(vmem_limit_bytes=mib << 20)


def on_core(core):
    return lax.axis_index("blk") % 2 == core


def halves(x):
    high = x.astype(BF16)
    return high, (x - high.astype(F32)).astype(BF16)


def product(a, b, dims):
    along_a, along_b = dims[0][0][0], dims[0][1][0]
    left = jnp.concatenate([a[0], a[0], a[1]], along_a)
    right = jnp.concatenate([b[0], b[1], b[0]], along_b)
    return lax.dot_general(left, right, dims, preferred_element_type=F32)


def tables(cnt, neg, mask, base_ref, slope_ref):
    rows, tiles = cnt.shape[0], mask.shape[0]
    tile = rows // tiles
    scale = 0.125 / math.sqrt(rows)
    columns = jnp.transpose(neg.astype(F32)).astype(jnp.int32)
    for row in range(0, rows, CHUNK):
        here, ti = slice(row, row + CHUNK), row // tile
        picks = [jnp.broadcast_to(columns[here, k : k + 1], (CHUNK, tile)) for k in range(neg.shape[0])]
        for tj in range(tiles):
            there = slice(tj * tile, (tj + 1) * tile)
            column = lax.broadcasted_iota(jnp.int32, (CHUNK, tile), 1) + tj * tile
            negcount = sum((pick == column).astype(F32) for pick in picks)
            count = cnt[here, there].astype(F32)
            gate = jnp.broadcast_to(mask[ti : ti + 1, tj : tj + 1].astype(F32) * scale, (CHUNK, tile))
            base_ref[here, there] = (count - negcount) * gate
            slope_ref[here, there] = (count + negcount) * gate


def packed_rows(rows, negs, tiles, steps):
    return -(-steps * (rows + negs + tiles) // 8) * 8


def tables_from(pack, index, steps, negs, tiles, base_ref, slope_ref):
    rows = pack.shape[1]
    at_neg = steps * rows + index * negs
    at_mask = steps * (rows + negs) + index * tiles
    tables(
        pack.at[index * rows : (index + 1) * rows],
        pack[at_neg : at_neg + negs],
        pack[at_mask : at_mask + tiles, :tiles],
        base_ref,
        slope_ref,
    )


def fill_pack(pack, first, steps, neg, mask):
    negs, tiles, rows = neg.shape[0], mask.shape[0], pack.shape[1]
    for i in range(steps):
        at_neg = steps * rows + i * negs
        at_mask = steps * (rows + negs) + i * tiles
        pack[at_neg : at_neg + negs] = neg[:, first + i]
        pack[at_mask : at_mask + tiles, :tiles] = mask[:, first + i]


def pass_body(vert, ctx, base, slope):
    vs, cs = halves(vert), halves(ctx)
    coef = base - slope * jnp.tanh(0.5 * product(vs, cs, NT))
    new_ctx = ctx + product(halves(jnp.transpose(coef)), vs, NN)
    new_vert = vert + product(halves(coef), cs, NN)
    return new_vert, new_ctx


def first_kernel(
    core, kept, vert_hbm, ctx_hbm, counts_hbm, neg_hbm, mask_hbm, *refs
):
    new_vert_ref, new_ctx_ref, near, far, vert, ctx, cnt, neg, mask, base, slope, sems = refs[kept:]

    @pl.when(on_core(core))
    def _():
        rows = cnt.shape[0]
        pairs = [
            (neg_hbm, neg),
            (mask_hbm, mask),
            (counts_hbm.at[0], cnt),
            (vert_hbm, vert),
            (ctx_hbm, ctx),
            (counts_hbm.at[1], near.at[:rows]),
            (counts_hbm.at[2], far.at[:rows]),
            (counts_hbm.at[3], far.at[rows : 2 * rows]),
        ]
        copies = [pltpu.make_async_copy(source, target, sems.at[i]) for i, (source, target) in enumerate(pairs)]
        for copy in copies:
            copy.start()
        for copy in copies[:5]:
            copy.wait()
        tables(cnt, neg[:, 0], mask[:, 0], base, slope)
        new_vert_ref[...], new_ctx_ref[...] = pass_body(vert[...], ctx[...], base[...], slope[...])
        fill_pack(near, 1, 1, neg, mask)
        fill_pack(far, 2, 2, neg, mask)
        for copy in copies[5:]:
            copy.wait()


def near_kernel(negs, tiles, after, near, base_ref, slope_ref):
    tables_from(near, 0, 1, negs, tiles, base_ref, slope_ref)


def far_kernel(negs, tiles, after, own, mate, base2, slope2, mate_base3, mate_slope3, own_base3, own_slope3):
    tables_from(mate, 0, 2, negs, tiles, base2, slope2)

    @pl.when(on_core(1))
    def _():
        tables_from(own, 1, 2, negs, tiles, own_base3, own_slope3)
        tables_from(mate, 1, 2, negs, tiles, mate_base3, mate_slope3)


def pass_kernel(core, after, vert_ref, ctx_ref, base_ref, slope_ref, new_vert_ref, new_ctx_ref):
    @pl.when(on_core(core))
    def _():
        new_vert_ref[...], new_ctx_ref[...] = pass_body(vert_ref[...], ctx_ref[...], base_ref[...], slope_ref[...])


def store_kernel(even_vert, even_ctx, odd_vert, odd_ctx, vert_hbm, ctx_hbm, sems):
    for core, (vert, ctx) in enumerate(((even_vert, even_ctx), (odd_vert, odd_ctx))):

        @pl.when(on_core(core))
        def _(vert=vert, ctx=ctx):
            copies = [pltpu.make_async_copy(vert, vert_hbm, sems.at[0]), pltpu.make_async_copy(ctx, ctx_hbm, sems.at[1])]
            for copy in copies:
                copy.start()
            for copy in copies:
                copy.wait()


def on_device(vertex_embed, context_embed, counts, negatives, masks):
    part, rows = vertex_embed.shape, counts.shape[1]
    negs, tiles = negatives.shape[1], masks.shape[1]
    vertex_embed, context_embed, counts = in_hbm(vertex_embed), in_hbm(context_embed), in_hbm(counts)
    negatives = in_hbm(jnp.transpose(negatives, (1, 0, 2)))
    masks = in_hbm(jnp.transpose(masks, (1, 0, 2)))
    state = pltpu.VMEM(part, F32)
    square = pltpu.VMEM((rows, rows), F32)
    small = [pltpu.VMEM(negatives.shape, jnp.int32), pltpu.VMEM(masks.shape, jnp.int32)]
    packs = [pltpu.VMEM((packed_rows(rows, negs, tiles, steps), rows), jnp.int32) for steps in (1, 2)]

    def call(kernel, outs, arrays, in_specs=None, **kwargs):
        return pl.pallas_call(
            kernel,
            out_shape=tuple(outs),
            in_specs=in_specs or [ANY_SPEC] + [VMEM_SPEC] * (len(arrays) - 1),
            out_specs=(VMEM_SPEC,) * len(outs),
            compiler_params=params(20),
            **kwargs,
        )(*arrays)

    def first(core, *kept):
        arrays = (vertex_embed, context_embed, counts, negatives, masks, *map(in_vmem, kept))
        return call(
            functools.partial(first_kernel, core, len(kept)),
            (state, state, *packs),
            arrays,
            [HBM_SPEC] * 5 + [VMEM_SPEC] * len(kept),
            scratch_shapes=[state, state, pltpu.VMEM((rows, rows), jnp.int32), *small, square, square, pltpu.SemaphoreType.DMA((8,))],
            input_output_aliases={5 + i: 2 + i for i in range(len(kept))},
        )

    def one_pass(core, after, vert, ctx, base, slope):
        arrays = (after, *map(in_vmem, (vert, ctx, base, slope)))
        return call(functools.partial(pass_kernel, core), (state, state), arrays)

    n_grp, n_blk = lax.axis_size("grp"), lax.axis_size("blk")

    def moved(value, core, blocks, swap=False):
        pairs = [
            (g * n_blk + b, (g ^ swap) * n_blk + (b + blocks) % n_blk) for g in range(n_grp) for b in range(core, n_blk, 2)
        ]
        return lax.ppermute(value, ("grp", "blk"), pairs)

    vert_o, out, *packed = first(1)
    outer0 = moved(out, 1, 1)
    vert_e, out, near, far = first(0, *packed)
    inner0 = moved(out, 0, 1)
    mate = lax.ppermute(far, "blk", [(b, b ^ 1) for b in range(n_blk)])
    table1 = call(functools.partial(near_kernel, negs, tiles), (square,) * 2, (vert_e, in_vmem(near)))
    vert_o, out = one_pass(1, table1[0], vert_o, inner0, *table1)
    swap1 = moved(vert_o, 1, -1, True)
    outer1 = moved(out, 1, 2)
    vert_e, out = one_pass(0, vert_o, vert_e, outer0, *table1)
    swap0 = moved(vert_e, 0, 1, True)
    far_tables = call(functools.partial(far_kernel, negs, tiles), (square,) * 6, (vert_e, in_vmem(far), in_vmem(mate)))
    table2, even3, odd3 = far_tables[:2], far_tables[2:4], far_tables[4:]
    vert_o, out = one_pass(0, table2[0], swap1, out, *table2)
    lend = moved(vert_o, 0, 1)
    outer2 = moved(out, 0, 3)
    vert_e, out = one_pass(1, vert_o, swap0, outer1, *table2)
    vert_o, out = one_pass(1, vert_e, lend, out, *odd3)
    outer3 = moved(out, 1, 1)
    vert_e, out = one_pass(1, vert_o, vert_e, outer2, *even3)
    back = moved(vert_e, 1, -1)
    return pl.pallas_call(
        store_kernel,
        out_shape=(pltpu.HBM(part, F32),) * 2,
        in_specs=[VMEM_SPEC] * 4,
        out_specs=(HBM_SPEC,) * 2,
        scratch_shapes=[pltpu.SemaphoreType.DMA((2,))],
        compiler_params=params(4),
        name="store",
    )(*map(in_vmem, (back, outer3, vert_o, out)))


def solution(mesh):
    placed = (
        P(("grp", "blk"), None),
        P(("grp", "blk"), None),
        P(None, ("grp", "blk"), None),
        P(None, None, ("grp", "blk")),
        P(None, ("grp", "blk"), None),
    )

    return jax.shard_map(
        on_device,
        mesh=mesh,
        in_specs=placed,
        out_specs=(P(("grp", "blk"), None), P(("grp", "blk"), None)),
        check_vma=False,
    )
```

```python
import functools
import math

import jax
import jax.numpy as jnp
from jax import lax
from jax.experimental import pallas as pl
from jax.experimental.pallas import tpu as pltpu
from jax.sharding import PartitionSpec as P


F32 = jnp.float32
BF16 = jnp.bfloat16
NT = (((1,), (1,)), ((), ()))
NN = (((1,), (0,)), ((), ()))
CHUNK = 32

VMEM_SPEC = pl.BlockSpec(memory_space=pltpu.VMEM)
HBM_SPEC = pl.BlockSpec(memory_space=pltpu.HBM)
ANY_SPEC = pl.BlockSpec(memory_space=pl.ANY)


def in_vmem(x):
    return pltpu.with_memory_space_constraint(x, pltpu.VMEM)


def in_hbm(x):
    return pltpu.with_memory_space_constraint(x, pltpu.HBM)


def params(mib):
    return pltpu.CompilerParams(vmem_limit_bytes=mib << 20)


def on_core(core):
    return lax.axis_index("blk") % 2 == core


def halves(x):
    high = x.astype(BF16)
    return high, (x - high.astype(F32)).astype(BF16)


def product(a, b, dims):
    along_a, along_b = dims[0][0][0], dims[0][1][0]
    left = jnp.concatenate([a[0], a[0], a[1]], along_a)
    right = jnp.concatenate([b[0], b[1], b[0]], along_b)
    return lax.dot_general(left, right, dims, preferred_element_type=F32)


def tables(cnt, neg, mask, base_ref, slope_ref):
    rows, tiles = cnt.shape[0], mask.shape[0]
    tile = rows // tiles
    scale = 0.125 / math.sqrt(rows)
    columns = jnp.transpose(neg.astype(F32)).astype(jnp.int32)
    for row in range(0, rows, CHUNK):
        here, ti = slice(row, row + CHUNK), row // tile
        picks = [jnp.broadcast_to(columns[here, k : k + 1], (CHUNK, tile)) for k in range(neg.shape[0])]
        for tj in range(tiles):
            there = slice(tj * tile, (tj + 1) * tile)
            column = lax.broadcasted_iota(jnp.int32, (CHUNK, tile), 1) + tj * tile
            negcount = sum((pick == column).astype(F32) for pick in picks)
            count = cnt[here, there].astype(F32)
            gate = jnp.broadcast_to(mask[ti : ti + 1, tj : tj + 1].astype(F32) * scale, (CHUNK, tile))
            base_ref[here, there] = (count - negcount) * gate
            slope_ref[here, there] = (count + negcount) * gate


def packed_rows(rows, negs, tiles, steps):
    return -(-steps * (rows + negs + tiles) // 8) * 8


def tables_from(pack, index, steps, negs, tiles, base_ref, slope_ref):
    rows = pack.shape[1]
    at_neg = steps * rows + index * negs
    at_mask = steps * (rows + negs) + index * tiles
    tables(
        pack.at[index * rows : (index + 1) * rows],
        pack[at_neg : at_neg + negs],
        pack[at_mask : at_mask + tiles, :tiles],
        base_ref,
        slope_ref,
    )


def fill_pack(pack, first, steps, neg, mask):
    negs, tiles, rows = neg.shape[0], mask.shape[0], pack.shape[1]
    for i in range(steps):
        at_neg = steps * rows + i * negs
        at_mask = steps * (rows + negs) + i * tiles
        pack[at_neg : at_neg + negs] = neg[:, first + i]
        pack[at_mask : at_mask + tiles, :tiles] = mask[:, first + i]


def pass_body(vert, ctx, base, slope):
    vs, cs = halves(vert), halves(ctx)
    coef = base - slope * jnp.tanh(0.5 * product(vs, cs, NT))
    new_ctx = ctx + product(halves(jnp.transpose(coef)), vs, NN)
    new_vert = vert + product(halves(coef), cs, NN)
    return new_vert, new_ctx


def first_kernel(
    core, kept, vert_hbm, ctx_hbm, counts_hbm, neg_hbm, mask_hbm, *refs
):
    new_vert_ref, new_ctx_ref, near, far, vert, ctx, cnt, neg, mask, base, slope, sems = refs[kept:]

    @pl.when(on_core(core))
    def _():
        rows = cnt.shape[0]
        pairs = [
            (neg_hbm, neg),
            (mask_hbm, mask),
            (counts_hbm.at[0], cnt),
            (vert_hbm, vert),
            (ctx_hbm, ctx),
            (counts_hbm.at[1], near.at[:rows]),
            (counts_hbm.at[2], far.at[:rows]),
            (counts_hbm.at[3], far.at[rows : 2 * rows]),
        ]
        copies = [pltpu.make_async_copy(source, target, sems.at[i]) for i, (source, target) in enumerate(pairs)]
        for copy in copies:
            copy.start()
        for copy in copies[:5]:
            copy.wait()
        tables(cnt, neg[:, 0], mask[:, 0], base, slope)
        new_vert_ref[...], new_ctx_ref[...] = pass_body(vert[...], ctx[...], base[...], slope[...])
        fill_pack(near, 1, 1, neg, mask)
        fill_pack(far, 2, 2, neg, mask)
        for copy in copies[5:]:
            copy.wait()


def near_kernel(negs, tiles, after, near, base_ref, slope_ref):
    tables_from(near, 0, 1, negs, tiles, base_ref, slope_ref)


def far_kernel(negs, tiles, after, own, from_even, from_odd, base2, slope2, own_base3, own_slope3):
    @pl.when(on_core(0))
    def _():
        tables_from(from_odd, 0, 2, negs, tiles, base2, slope2)

    @pl.when(on_core(1))
    def _():
        tables_from(from_even, 0, 2, negs, tiles, base2, slope2)
        tables_from(own, 1, 2, negs, tiles, own_base3, own_slope3)


def last_kernel(negs, tiles, after, from_even, base_ref, slope_ref):
    @pl.when(on_core(1))
    def _():
        tables_from(from_even, 1, 2, negs, tiles, base_ref, slope_ref)


def pass_kernel(core, after, vert_ref, ctx_ref, base_ref, slope_ref, new_vert_ref, new_ctx_ref):
    @pl.when(on_core(core))
    def _():
        new_vert_ref[...], new_ctx_ref[...] = pass_body(vert_ref[...], ctx_ref[...], base_ref[...], slope_ref[...])


def store_kernel(core, vert, ctx, *refs):
    vert_hbm, ctx_hbm, sems = refs[-3:]

    @pl.when(on_core(core))
    def _():
        copies = [pltpu.make_async_copy(vert, vert_hbm, sems.at[0]), pltpu.make_async_copy(ctx, ctx_hbm, sems.at[1])]
        for copy in copies:
            copy.start()
        for copy in copies:
            copy.wait()


def on_device(vertex_embed, context_embed, counts, negatives, masks):
    part, rows = vertex_embed.shape, counts.shape[1]
    negs, tiles = negatives.shape[1], masks.shape[1]
    vertex_embed, context_embed, counts = in_hbm(vertex_embed), in_hbm(context_embed), in_hbm(counts)
    negatives = in_hbm(jnp.transpose(negatives, (1, 0, 2)))
    masks = in_hbm(jnp.transpose(masks, (1, 0, 2)))
    state = pltpu.VMEM(part, F32)
    square = pltpu.VMEM((rows, rows), F32)
    small = [pltpu.VMEM(negatives.shape, jnp.int32), pltpu.VMEM(masks.shape, jnp.int32)]
    packs = [pltpu.VMEM((packed_rows(rows, negs, tiles, steps), rows), jnp.int32) for steps in (1, 2)]

    def call(kernel, outs, arrays, in_specs=None, **kwargs):
        return pl.pallas_call(
            kernel,
            out_shape=tuple(outs),
            in_specs=in_specs or [ANY_SPEC] + [VMEM_SPEC] * (len(arrays) - 1),
            out_specs=(VMEM_SPEC,) * len(outs),
            compiler_params=params(20),
            **kwargs,
        )(*arrays)

    def first(core, *kept):
        arrays = (vertex_embed, context_embed, counts, negatives, masks, *map(in_vmem, kept))
        return call(
            functools.partial(first_kernel, core, len(kept)),
            (state, state, *packs),
            arrays,
            [HBM_SPEC] * 5 + [VMEM_SPEC] * len(kept),
            scratch_shapes=[state, state, pltpu.VMEM((rows, rows), jnp.int32), *small, square, square, pltpu.SemaphoreType.DMA((8,))],
            input_output_aliases={5 + i: 2 + i for i in range(len(kept))},
        )

    def one_pass(core, after, vert, ctx, base, slope):
        arrays = (after, *map(in_vmem, (vert, ctx, base, slope)))
        return call(functools.partial(pass_kernel, core), (state, state), arrays)

    n_grp, n_blk = lax.axis_size("grp"), lax.axis_size("blk")

    def moved(value, core, blocks, swap=False):
        pairs = [
            (g * n_blk + b, (g ^ swap) * n_blk + (b + blocks) % n_blk) for g in range(n_grp) for b in range(core, n_blk, 2)
        ]
        return lax.ppermute(value, ("grp", "blk"), pairs)

    def store(core, vert, ctx, *stored):
        return pl.pallas_call(
            functools.partial(store_kernel, core),
            out_shape=(pltpu.HBM(part, F32),) * 2,
            in_specs=[VMEM_SPEC] * 2 + [HBM_SPEC] * len(stored),
            out_specs=(HBM_SPEC,) * 2,
            scratch_shapes=[pltpu.SemaphoreType.DMA((2,))],
            input_output_aliases={2 + i: i for i in range(len(stored))},
            compiler_params=params(4),
        )(*map(in_vmem, (vert, ctx)), *stored)

    vert_o, out, *packed = first(1)
    outer0 = moved(out, 1, 1)
    vert_e, out, near, far = first(0, *packed)
    inner0 = moved(out, 0, 1)
    from_even = moved(far, 0, 1)
    table1 = call(functools.partial(near_kernel, negs, tiles), (square,) * 2, (vert_e, in_vmem(near)))
    vert_o, out = one_pass(1, table1[0], vert_o, inner0, *table1)
    swap1 = moved(vert_o, 1, -1, True)
    from_odd = moved(far, 1, -1)
    outer1 = moved(out, 1, 2)
    vert_e, out = one_pass(0, vert_o, vert_e, outer0, *table1)
    swap0 = moved(vert_e, 0, 1, True)
    arrays = (vert_e, *map(in_vmem, (far, from_even, from_odd)))
    far_tables = call(functools.partial(far_kernel, negs, tiles), (square,) * 4, arrays)
    table2, odd3 = far_tables[:2], far_tables[2:]
    vert_o, out = one_pass(0, table2[0], swap1, out, *table2)
    lend = moved(vert_o, 0, 1)
    outer2 = moved(out, 0, 3)
    vert_e, out = one_pass(1, vert_o, swap0, outer1, *table2)
    vert_o, out = one_pass(1, vert_e, lend, out, *odd3)
    outer3 = moved(out, 1, 1)
    even3 = call(functools.partial(last_kernel, negs, tiles), (square,) * 2, (vert_o, in_vmem(from_even)))
    vert_e, out = one_pass(1, even3[0], vert_e, outer2, *even3)
    back = moved(vert_e, 1, -1)
    stored = store(1, vert_o, out)
    return tuple(store(0, back, outer3, *stored))


def solution(mesh):
    placed = (
        P(("grp", "blk"), None),
        P(("grp", "blk"), None),
        P(None, ("grp", "blk"), None),
        P(None, None, ("grp", "blk")),
        P(None, ("grp", "blk"), None),
    )

    return jax.shard_map(
        on_device,
        mesh=mesh,
        in_specs=placed,
        out_specs=(P(("grp", "blk"), None), P(("grp", "blk"), None)),
        check_vma=False,
    )
```

```python
import functools
import math

import jax
import jax.numpy as jnp
from jax import lax
from jax.experimental import pallas as pl
from jax.experimental.pallas import tpu as pltpu
from jax.sharding import PartitionSpec as P


F32 = jnp.float32
BF16 = jnp.bfloat16
NT = (((1,), (1,)), ((), ()))
NN = (((1,), (0,)), ((), ()))
CHUNK = 32

VMEM_SPEC = pl.BlockSpec(memory_space=pltpu.VMEM)
HBM_SPEC = pl.BlockSpec(memory_space=pltpu.HBM)
ANY_SPEC = pl.BlockSpec(memory_space=pl.ANY)


def in_vmem(x):
    return pltpu.with_memory_space_constraint(x, pltpu.VMEM)


def in_hbm(x):
    return pltpu.with_memory_space_constraint(x, pltpu.HBM)


def params(mib):
    return pltpu.CompilerParams(vmem_limit_bytes=mib << 20)


def on_core(core):
    return lax.axis_index("blk") % 2 == core


def halves(x):
    high = x.astype(BF16)
    return high, (x - high.astype(F32)).astype(BF16)


def product(a, b, dims):
    along_a, along_b = dims[0][0][0], dims[0][1][0]
    left = jnp.concatenate([a[0], a[0], a[1]], along_a)
    right = jnp.concatenate([b[0], b[1], b[0]], along_b)
    return lax.dot_general(left, right, dims, preferred_element_type=F32)


def tables(block, neg, mask, base_ref, slope_ref):
    rows, tiles = base_ref.shape[0], mask.shape[0]
    tile = rows // tiles
    scale = 0.125 / math.sqrt(rows)
    columns = jnp.transpose(neg.astype(F32)).astype(jnp.int32)
    for row in range(0, rows, CHUNK):
        here, ti = slice(row, row + CHUNK), row // tile
        picks = [jnp.broadcast_to(columns[here, k : k + 1], (CHUNK, tile)) for k in range(neg.shape[0])]
        for tj in range(tiles):
            there = slice(tj * tile, (tj + 1) * tile)
            column = lax.broadcasted_iota(jnp.int32, (CHUNK, tile), 1) + tj * tile
            negcount = sum((pick == column).astype(F32) for pick in picks)
            count = block(here, there).astype(F32)
            gate = jnp.broadcast_to(mask[ti : ti + 1, tj : tj + 1].astype(F32) * scale, (CHUNK, tile))
            base_ref[here, there] = (count - negcount) * gate
            slope_ref[here, there] = (count + negcount) * gate


def packed_rows(rows, negs, tiles, steps):
    return -(-steps * (rows + negs + tiles) // 8) * 8


def pack_parts(pack, index, steps, negs, tiles):
    rows = pack.shape[1]
    at_neg = steps * rows + index * negs
    at_mask = steps * (rows + negs) + index * tiles
    counts = pack.at[index * rows : (index + 1) * rows]
    return counts, pack[at_neg : at_neg + negs], pack[at_mask : at_mask + tiles, :tiles]


def tables_from(pack, index, steps, negs, tiles, base_ref, slope_ref):
    counts, neg, mask = pack_parts(pack, index, steps, negs, tiles)
    tables(lambda here, there: counts[here, there], neg, mask, base_ref, slope_ref)


def folded_places(rows, width, negs, tiles):
    half, rest = rows // 2, rows - width
    first, second = slice(0, width), slice(width, rows)
    counts = [
        ((slice(0, rows), first), (slice(0, rows), first)),
        ((slice(rows, rows + half), slice(0, rest)), (slice(0, half), second)),
        ((slice(rows, rows + half), slice(rest, 2 * rest)), (slice(half, rows), second)),
    ]
    top = rows + half
    neg = [(slice(top, top + negs), first), (slice(top + negs, top + 2 * negs), slice(0, rest))]
    mask = (slice(top + 2 * negs, top + 2 * negs + tiles), slice(0, tiles))
    return counts, neg, mask


def folded_rows(rows, negs, tiles):
    return -(-(rows + rows // 2 + 2 * negs + tiles) // 8) * 8


def fold(pack, steps, negs, tiles, folded):
    counts, neg, mask = pack_parts(pack, 0, steps, negs, tiles)
    rows, width = pack.shape[1], folded.shape[1]
    at_counts, at_neg, at_mask = folded_places(rows, width, negs, tiles)
    for there, here in at_counts:
        folded[there] = counts[here].astype(F32)
    folded[at_neg[0]] = neg[:, :width].astype(F32)
    folded[at_neg[1]] = neg[:, width:].astype(F32)
    folded[at_mask] = mask.astype(F32)


def tables_folded(folded, rows, negs, tiles, base_ref, slope_ref):
    width, half = folded.shape[1], rows // 2
    _, at_neg, at_mask = folded_places(rows, width, negs, tiles)

    def block(here, there):
        if there.stop <= width:
            return folded[here, there]
        low = here.stop <= half
        row = rows + here.start - (0 if low else half)
        column = there.start - width + (0 if low else rows - width)
        return folded[row : row + CHUNK, column : column + there.stop - there.start]

    neg = jnp.concatenate([folded[at_neg[0]], folded[at_neg[1]]], 1)
    tables(block, neg, folded[at_mask], base_ref, slope_ref)


def fill_pack(pack, first, steps, neg, mask):
    negs, tiles, rows = neg.shape[0], mask.shape[0], pack.shape[1]
    for i in range(steps):
        at_neg = steps * rows + i * negs
        at_mask = steps * (rows + negs) + i * tiles
        pack[at_neg : at_neg + negs] = neg[:, first + i]
        pack[at_mask : at_mask + tiles, :tiles] = mask[:, first + i]


def pass_body(vert, ctx, base, slope):
    vs, cs = halves(vert), halves(ctx)
    coef = base - slope * jnp.tanh(0.5 * product(vs, cs, NT))
    new_ctx = ctx + product(halves(jnp.transpose(coef)), vs, NN)
    new_vert = vert + product(halves(coef), cs, NN)
    return new_vert, new_ctx


def first_kernel(core, kept, vert_hbm, ctx_hbm, counts_hbm, neg_hbm, mask_hbm, *refs):
    new_vert_ref, new_ctx_ref, near, far, vert, ctx, cnt, neg, mask, base, slope, sems = refs[kept:]
    rows, negs, tiles = cnt.shape[0], neg.shape[0], mask.shape[0]

    @pl.when(on_core(core))
    def _():
        pairs = [
            (neg_hbm, neg),
            (mask_hbm, mask),
            (counts_hbm.at[0], cnt),
            (vert_hbm, vert),
            (ctx_hbm, ctx),
            (counts_hbm.at[1], near.at[:rows]),
            (counts_hbm.at[2], far.at[:rows]),
            (counts_hbm.at[3], far.at[rows : 2 * rows]),
        ]
        copies = [pltpu.make_async_copy(source, target, sems.at[i]) for i, (source, target) in enumerate(pairs)]
        for copy in copies:
            copy.start()
        for copy in copies[:5]:
            copy.wait()
        tables(lambda here, there: cnt[here, there], neg[:, 0], mask[:, 0], base, slope)
        new_vert_ref[...], new_ctx_ref[: vert.shape[0]] = pass_body(vert[...], ctx[...], base[...], slope[...])
        fill_pack(near, 1, 1, neg, mask)
        fill_pack(far, 2, 2, neg, mask)
        for copy in copies[5:]:
            copy.wait()

    if core == 0:

        @pl.when(on_core(1))
        def _():
            fold(far, 2, negs, tiles, new_ctx_ref)


def near_kernel(core, negs, tiles, after, near, base_ref, slope_ref):
    @pl.when(on_core(core))
    def _():
        tables_from(near, 0, 1, negs, tiles, base_ref, slope_ref)


def far_kernel(negs, tiles, after, own, from_even, from_odd, base2, slope2, own_base3, own_slope3):
    @pl.when(on_core(0))
    def _():
        tables_folded(from_odd, own.shape[1], negs, tiles, base2, slope2)

    @pl.when(on_core(1))
    def _():
        tables_from(from_even, 0, 2, negs, tiles, base2, slope2)
        tables_from(own, 1, 2, negs, tiles, own_base3, own_slope3)


def last_kernel(negs, tiles, after, from_even, base_ref, slope_ref):
    @pl.when(on_core(1))
    def _():
        tables_from(from_even, 1, 2, negs, tiles, base_ref, slope_ref)


def pass_kernel(core, after, vert_ref, ctx_ref, base_ref, slope_ref, new_vert_ref, new_ctx_ref):
    @pl.when(on_core(core))
    def _():
        new_vert_ref[...], new_ctx_ref[...] = pass_body(
            vert_ref[...], ctx_ref[: vert_ref.shape[0]], base_ref[...], slope_ref[...]
        )


def store_kernel(core, vert, ctx, *refs):
    vert_hbm, ctx_hbm, sems = refs[-3:]

    @pl.when(on_core(core))
    def _():
        copies = [pltpu.make_async_copy(vert, vert_hbm, sems.at[0]), pltpu.make_async_copy(ctx, ctx_hbm, sems.at[1])]
        for copy in copies:
            copy.start()
        for copy in copies:
            copy.wait()


def on_device(vertex_embed, context_embed, counts, negatives, masks):
    part, rows = vertex_embed.shape, counts.shape[1]
    negs, tiles = negatives.shape[1], masks.shape[1]
    vertex_embed, context_embed, counts = in_hbm(vertex_embed), in_hbm(context_embed), in_hbm(counts)
    negatives = in_hbm(jnp.transpose(negatives, (1, 0, 2)))
    masks = in_hbm(jnp.transpose(masks, (1, 0, 2)))
    state = pltpu.VMEM(part, F32)
    square = pltpu.VMEM((rows, rows), F32)
    small = [pltpu.VMEM(negatives.shape, jnp.int32), pltpu.VMEM(masks.shape, jnp.int32)]
    folded = pltpu.VMEM((folded_rows(rows, negs, tiles), part[1]), F32)
    packs = [pltpu.VMEM((packed_rows(rows, negs, tiles, steps), rows), jnp.int32) for steps in (1, 2)]

    def call(kernel, outs, arrays, in_specs=None, **kwargs):
        return pl.pallas_call(
            kernel,
            out_shape=tuple(outs),
            in_specs=in_specs or [ANY_SPEC] + [VMEM_SPEC] * (len(arrays) - 1),
            out_specs=(VMEM_SPEC,) * len(outs),
            compiler_params=params(20),
            **kwargs,
        )(*arrays)

    def first(core, *kept):
        arrays = (vertex_embed, context_embed, counts, negatives, masks, *map(in_vmem, kept))
        return call(
            functools.partial(first_kernel, core, len(kept)),
            (state, state if core else folded, *packs),
            arrays,
            [HBM_SPEC] * 5 + [VMEM_SPEC] * len(kept),
            scratch_shapes=[state, state, pltpu.VMEM((rows, rows), jnp.int32), *small, square, square, pltpu.SemaphoreType.DMA((8,))],
            input_output_aliases={5 + i: 2 + i for i in range(len(kept))},
        )

    def one_pass(core, after, vert, ctx, base, slope):
        arrays = (after, *map(in_vmem, (vert, ctx, base, slope)))
        return call(functools.partial(pass_kernel, core), (state, state), arrays)

    n_grp, n_blk = lax.axis_size("grp"), lax.axis_size("blk")

    def moved(value, core, blocks, swap=False):
        pairs = [
            (g * n_blk + b, (g ^ swap) * n_blk + (b + blocks) % n_blk) for g in range(n_grp) for b in range(core, n_blk, 2)
        ]
        return lax.ppermute(value, ("grp", "blk"), pairs)

    def store(core, vert, ctx, *stored):
        return pl.pallas_call(
            functools.partial(store_kernel, core),
            out_shape=(pltpu.HBM(part, F32),) * 2,
            in_specs=[VMEM_SPEC] * 2 + [HBM_SPEC] * len(stored),
            out_specs=(HBM_SPEC,) * 2,
            scratch_shapes=[pltpu.SemaphoreType.DMA((2,))],
            input_output_aliases={2 + i: i for i in range(len(stored))},
            compiler_params=params(4),
        )(*map(in_vmem, (vert, ctx)), *stored)

    vert_o, out, *packed = first(1)
    outer0 = moved(out, 1, 1)
    vert_e, out, near, far = first(0, *packed)
    inner0 = lax.ppermute(out, "blk", [(b, b ^ 1) for b in range(n_blk)])
    from_even = moved(far, 0, 1)
    table1 = call(functools.partial(near_kernel, 1, negs, tiles), (square,) * 2, (vert_e, in_vmem(near)))
    vert_o, out = one_pass(1, table1[0], vert_o, inner0, *table1)
    swap1 = moved(vert_o, 1, -1, True)
    outer1 = moved(out, 1, 2)
    table1 = call(functools.partial(near_kernel, 0, negs, tiles), (square,) * 2, (vert_o, in_vmem(near)))
    vert_e, out = one_pass(0, table1[0], vert_e, outer0, *table1)
    swap0 = moved(vert_e, 0, 1, True)
    arrays = (vert_e, *map(in_vmem, (far, from_even, inner0)))
    far_tables = call(functools.partial(far_kernel, negs, tiles), (square,) * 4, arrays)
    table2, odd3 = far_tables[:2], far_tables[2:]
    vert_o, out = one_pass(0, table2[0], swap1, out, *table2)
    lend = moved(vert_o, 0, 1)
    outer2 = moved(out, 0, 3)
    vert_e, out = one_pass(1, vert_o, swap0, outer1, *table2)
    vert_o, out = one_pass(1, vert_e, lend, out, *odd3)
    outer3 = moved(out, 1, 1)
    even3 = call(functools.partial(last_kernel, negs, tiles), (square,) * 2, (vert_o, in_vmem(from_even)))
    vert_e, out = one_pass(1, even3[0], vert_e, outer2, *even3)
    back = moved(vert_e, 1, -1)
    stored = store(1, vert_o, out)
    return tuple(store(0, back, outer3, *stored))


def solution(mesh):
    placed = (
        P(("grp", "blk"), None),
        P(("grp", "blk"), None),
        P(None, ("grp", "blk"), None),
        P(None, None, ("grp", "blk")),
        P(None, ("grp", "blk"), None),
    )

    return jax.shard_map(
        on_device,
        mesh=mesh,
        in_specs=placed,
        out_specs=(P(("grp", "blk"), None), P(("grp", "blk"), None)),
        check_vma=False,
    )
```

```python
import functools
import math

import jax
import jax.numpy as jnp
from jax import lax
from jax.experimental import pallas as pl
from jax.experimental.pallas import tpu as pltpu
from jax.sharding import PartitionSpec as P


F32 = jnp.float32
BF16 = jnp.bfloat16
NT = (((1,), (1,)), ((), ()))
NN = (((1,), (0,)), ((), ()))
CHUNK = 32

VMEM_SPEC = pl.BlockSpec(memory_space=pltpu.VMEM)
HBM_SPEC = pl.BlockSpec(memory_space=pltpu.HBM)
ANY_SPEC = pl.BlockSpec(memory_space=pl.ANY)


def in_vmem(x):
    return pltpu.with_memory_space_constraint(x, pltpu.VMEM)


def in_hbm(x):
    return pltpu.with_memory_space_constraint(x, pltpu.HBM)


def params(mib):
    return pltpu.CompilerParams(vmem_limit_bytes=mib << 20)


def on_core(core):
    return lax.axis_index("blk") % 2 == core


def halves(x):
    high = x.astype(BF16)
    return high, (x - high.astype(F32)).astype(BF16)


def product(a, b, dims):
    along_a, along_b = dims[0][0][0], dims[0][1][0]
    left = jnp.concatenate([a[0], a[0], a[1]], along_a)
    right = jnp.concatenate([b[0], b[1], b[0]], along_b)
    return lax.dot_general(left, right, dims, preferred_element_type=F32)


def row_product(a, b):
    left = jnp.concatenate([a[0], a[0], a[1]], 1)
    right = jnp.concatenate([b[0], b[1], b[0]], 0)
    half = left.shape[0] // 2
    dot = functools.partial(lax.dot_general, dimension_numbers=NN, preferred_element_type=F32)
    return jnp.concatenate([dot(left[:half], right), dot(left[half:], right)], 0)


def negcounts(block_rows, tile, tiles, neg):
    columns = jnp.transpose(neg.astype(F32)).astype(jnp.int32)
    for row in range(0, columns.shape[0], block_rows):
        here = slice(row, row + block_rows)
        picks = [jnp.broadcast_to(columns[here, k : k + 1], (block_rows, tile)) for k in range(neg.shape[0])]
        for tj in range(tiles):
            column = lax.broadcasted_iota(jnp.int32, (block_rows, tile), 1) + tj * tile
            yield here, slice(tj * tile, (tj + 1) * tile), sum((pick == column).astype(F32) for pick in picks)


def gate_of(mask, tile, scale):
    tiles = mask.shape[0]
    mask = mask.astype(F32) * scale
    spread = [[jnp.broadcast_to(mask[i : i + 1, j : j + 1], (tile, tile)) for j in range(tiles)] for i in range(tiles)]
    return jnp.concatenate([jnp.concatenate(row, 1) for row in spread], 0)


def tables(block, neg, mask, base_ref, slope_ref):
    rows, tiles = base_ref.shape[0], mask.shape[0]
    tile = rows // tiles
    scale = 0.125 / math.sqrt(rows)
    for here, there, negcount in negcounts(CHUNK, tile, tiles, neg):
        ti, tj = here.start // tile, there.start // tile
        count = block(here, there).astype(F32)
        gate = jnp.broadcast_to(mask[ti : ti + 1, tj : tj + 1].astype(F32) * scale, (CHUNK, tile))
        base_ref[here, there] = (count - negcount) * gate
        slope_ref[here, there] = (count + negcount) * gate


def packed_rows(rows, negs, tiles, steps):
    return -(-steps * (rows + negs + tiles) // 8) * 8


def pack_parts(pack, index, steps, negs, tiles):
    rows = pack.shape[1]
    at_neg = steps * rows + index * negs
    at_mask = steps * (rows + negs) + index * tiles
    counts = pack.at[index * rows : (index + 1) * rows]
    return counts, pack[at_neg : at_neg + negs], pack[at_mask : at_mask + tiles, :tiles]


def tables_from(pack, index, steps, negs, tiles, base_ref, slope_ref):
    counts, neg, mask = pack_parts(pack, index, steps, negs, tiles)
    tables(lambda here, there: counts[here, there], neg, mask, base_ref, slope_ref)


def folded_places(rows, width, negs, tiles):
    half, rest = rows // 2, rows - width
    first, second = slice(0, width), slice(width, rows)
    counts = [
        ((slice(0, rows), first), (slice(0, rows), first)),
        ((slice(rows, rows + half), slice(0, rest)), (slice(0, half), second)),
        ((slice(rows, rows + half), slice(rest, 2 * rest)), (slice(half, rows), second)),
    ]
    top = rows + half
    neg = [(slice(top, top + negs), first), (slice(top + negs, top + 2 * negs), slice(0, rest))]
    mask = (slice(top + 2 * negs, top + 2 * negs + tiles), slice(0, tiles))
    return counts, neg, mask


def folded_rows(rows, negs, tiles):
    return -(-(rows + rows // 2 + 2 * negs + tiles) // 8) * 8


def fold(pack, steps, negs, tiles, folded):
    counts, neg, mask = pack_parts(pack, 0, steps, negs, tiles)
    rows, width = pack.shape[1], folded.shape[1]
    at_counts, at_neg, at_mask = folded_places(rows, width, negs, tiles)
    for there, here in at_counts:
        folded[there] = counts[here].astype(F32)
    folded[at_neg[0]] = neg[:, :width].astype(F32)
    folded[at_neg[1]] = neg[:, width:].astype(F32)
    folded[at_mask] = mask.astype(F32)


def tables_folded(folded, rows, negs, tiles, base_ref, slope_ref):
    width, half = folded.shape[1], rows // 2
    _, at_neg, at_mask = folded_places(rows, width, negs, tiles)

    def block(here, there):
        if there.stop <= width:
            return folded[here, there]
        low = here.stop <= half
        row = rows + here.start - (0 if low else half)
        column = there.start - width + (0 if low else rows - width)
        return folded[row : row + CHUNK, column : column + there.stop - there.start]

    neg = jnp.concatenate([folded[at_neg[0]], folded[at_neg[1]]], 1)
    tables(block, neg, folded[at_mask], base_ref, slope_ref)


def fill_pack(pack, first, steps, neg, mask):
    negs, tiles, rows = neg.shape[0], mask.shape[0], pack.shape[1]
    for i in range(steps):
        at_neg = steps * rows + i * negs
        at_mask = steps * (rows + negs) + i * tiles
        pack[at_neg : at_neg + negs] = neg[:, first + i]
        pack[at_mask : at_mask + tiles, :tiles] = mask[:, first + i]


def pass_body(vert, ctx, base, slope):
    vs, cs = halves(vert), halves(ctx)
    coef = base - slope * jnp.tanh(0.5 * product(vs, cs, NT))
    new_ctx = ctx + product(halves(jnp.transpose(coef)), vs, NN)
    new_vert = vert + product(halves(coef), cs, NN)
    return new_vert, new_ctx


def context_part(vs, ctx, coef):
    return ctx + row_product(halves(jnp.transpose(coef)), vs)


def vertex_part(vert, ctx, coef):
    return vert + row_product(halves(coef), halves(ctx))


def first_kernel(core, kept, vert_hbm, ctx_hbm, counts_hbm, neg_hbm, mask_hbm, *refs):
    refs, (cnt, neg, mask, negcount, sems) = refs[:-5], refs[-5:]
    before, (near, far, vert, ctx, coef_ref, new_ctx_ref, *late) = refs[:kept], refs[kept:]
    rows, negs, tiles = cnt.shape[0], neg.shape[0], mask.shape[0]
    tile = rows // tiles

    @pl.when(on_core(core))
    def _():
        pairs = [
            (neg_hbm, neg),
            (mask_hbm, mask),
            (vert_hbm, vert),
            (ctx_hbm, ctx),
            (counts_hbm.at[0], cnt),
            (counts_hbm.at[1], near.at[:rows]),
            (counts_hbm.at[2], far.at[:rows]),
            (counts_hbm.at[3], far.at[rows : 2 * rows]),
        ]
        copies = [pltpu.make_async_copy(source, target, sems.at[i]) for i, (source, target) in enumerate(pairs)]
        for copy in copies:
            copy.start()
        copies[0].wait()
        for here, there, value in negcounts(CHUNK, tile, tiles, neg[:, 0]):
            negcount[here, there] = value
        for copy in copies[1:5]:
            copy.wait()
        vs, cs = halves(vert[...]), halves(ctx[...])
        tanh = jnp.tanh(0.5 * product(vs, cs, NT))
        count = cnt[...].astype(F32)
        gate = gate_of(mask[:, 0], tile, 0.125 / math.sqrt(rows))
        coef = gate * ((count - negcount[...]) - (count + negcount[...]) * tanh)
        coef_ref[...] = coef
        new_ctx_ref[: ctx.shape[0]] = context_part(vs, ctx[...], coef)
        fill_pack(near, 1, 1, neg, mask)
        fill_pack(far, 2, 2, neg, mask)
        for copy in copies[5:]:
            copy.wait()

    if core == 0:

        @pl.when(on_core(1))
        def _():
            fold(far, 2, negs, tiles, new_ctx_ref)
            late[0][...] = vertex_part(*(ref[...] for ref in before[2:]))


def odd_near_kernel(negs, tiles, after, near, base_ref, slope_ref):
    @pl.when(on_core(1))
    def _():
        tables_from(near, 0, 1, negs, tiles, base_ref, slope_ref)


def even_near_kernel(negs, tiles, after, near, from_odd, vert, ctx, coef, base1, slope1, base2, slope2, new_vert_ref):
    @pl.when(on_core(0))
    def _():
        tables_from(near, 0, 1, negs, tiles, base1, slope1)
        tables_folded(from_odd, near.shape[1], negs, tiles, base2, slope2)
        new_vert_ref[...] = vertex_part(vert[...], ctx[...], coef[...])


def odd_far_kernel(negs, tiles, after, own, from_even, base2, slope2, own_base3, own_slope3):
    @pl.when(on_core(1))
    def _():
        tables_from(from_even, 0, 2, negs, tiles, base2, slope2)
        tables_from(own, 1, 2, negs, tiles, own_base3, own_slope3)


def last_kernel(negs, tiles, after, from_even, vert2, ctx2, coef2, vert3, ctx3, coef3, base_ref, slope_ref, even_vert_ref, odd_vert_ref):
    @pl.when(on_core(1))
    def _():
        tables_from(from_even, 1, 2, negs, tiles, base_ref, slope_ref)
        even_vert_ref[...] = vertex_part(vert2[...], ctx2[...], coef2[...])
        odd_vert_ref[...] = vertex_part(vert3[...], ctx3[...], coef3[...])


def context_kernel(core, after, vert_ref, ctx_ref, base_ref, slope_ref, coef_ref, new_ctx_ref):
    @pl.when(on_core(core))
    def _():
        vs, cs = halves(vert_ref[...]), halves(ctx_ref[...])
        coef = base_ref[...] - slope_ref[...] * jnp.tanh(0.5 * product(vs, cs, NT))
        coef_ref[...] = coef
        new_ctx_ref[...] = context_part(vs, ctx_ref[...], coef)


def pass_kernel(core, after, vert_ref, ctx_ref, base_ref, slope_ref, new_vert_ref, new_ctx_ref):
    @pl.when(on_core(core))
    def _():
        new_vert_ref[...], new_ctx_ref[...] = pass_body(
            vert_ref[...], ctx_ref[: vert_ref.shape[0]], base_ref[...], slope_ref[...]
        )


def store_kernel(core, count, *refs):
    sources, targets, sems = refs[:count], refs[-1 - count : -1], refs[-1]

    @pl.when(on_core(core))
    def _():
        copies = [pltpu.make_async_copy(s, t, sems.at[i]) for i, (s, t) in enumerate(zip(sources, targets, strict=True))]
        for copy in copies:
            copy.start()
        for copy in copies:
            copy.wait()


def on_device(vertex_embed, context_embed, counts, negatives, masks):
    part, rows = vertex_embed.shape, counts.shape[1]
    negs, tiles = negatives.shape[1], masks.shape[1]
    vertex_embed, context_embed, counts = in_hbm(vertex_embed), in_hbm(context_embed), in_hbm(counts)
    negatives = in_hbm(jnp.transpose(negatives, (1, 0, 2)))
    masks = in_hbm(jnp.transpose(masks, (1, 0, 2)))
    state = pltpu.VMEM(part, F32)
    square = pltpu.VMEM((rows, rows), F32)
    small = [pltpu.VMEM(negatives.shape, jnp.int32), pltpu.VMEM(masks.shape, jnp.int32)]
    folded = pltpu.VMEM((folded_rows(rows, negs, tiles), part[1]), F32)
    packs = [pltpu.VMEM((packed_rows(rows, negs, tiles, steps), rows), jnp.int32) for steps in (1, 2)]

    def call(kernel, outs, arrays, in_specs=None, **kwargs):
        return pl.pallas_call(
            kernel,
            out_shape=tuple(outs),
            in_specs=in_specs or [ANY_SPEC] + [VMEM_SPEC] * (len(arrays) - 1),
            out_specs=(VMEM_SPEC,) * len(outs),
            compiler_params=params(20),
            **kwargs,
        )(*arrays)

    def first(core, *kept):
        arrays = (vertex_embed, context_embed, counts, negatives, masks, *map(in_vmem, kept))
        return call(
            functools.partial(first_kernel, core, len(kept)),
            (*packs, state, state, square) + ((state,) if core else (folded, state)),
            arrays,
            [HBM_SPEC] * 5 + [VMEM_SPEC] * len(kept),
            scratch_shapes=[pltpu.VMEM((rows, rows), jnp.int32), *small, square, pltpu.SemaphoreType.DMA((8,))],
            input_output_aliases={5 + i: i for i in range(len(kept[:2]))},
        )

    def context_pass(core, after, vert, ctx, base, slope):
        arrays = (after, *map(in_vmem, (vert, ctx, base, slope)))
        return call(functools.partial(context_kernel, core), (square, state), arrays)

    def one_pass(core, after, vert, ctx, base, slope):
        arrays = (after, *map(in_vmem, (vert, ctx, base, slope)))
        return call(functools.partial(pass_kernel, core), (state, state), arrays)

    n_grp, n_blk = lax.axis_size("grp"), lax.axis_size("blk")

    def moved(value, core, blocks, swap=False):
        pairs = [
            (g * n_blk + b, (g ^ swap) * n_blk + (b + blocks) % n_blk) for g in range(n_grp) for b in range(core, n_blk, 2)
        ]
        return lax.ppermute(value, ("grp", "blk"), pairs)

    def store(core, arrays, stored=()):
        count = len(arrays)
        return pl.pallas_call(
            functools.partial(store_kernel, core, count),
            out_shape=(pltpu.HBM(part, F32),) * count,
            in_specs=[VMEM_SPEC] * count + [HBM_SPEC] * len(stored),
            out_specs=(HBM_SPEC,) * count,
            scratch_shapes=[pltpu.SemaphoreType.DMA((count,))],
            input_output_aliases={count + i: i for i in range(len(stored))},
            compiler_params=params(4),
        )(*map(in_vmem, arrays), *stored)

    near, far, *start_o, out = first(1)
    outer0 = moved(out, 1, 1)
    near, far, *start_e, out, vert_o = first(0, near, far, *start_o)
    inner0 = lax.ppermute(out, "blk", [(b, b ^ 1) for b in range(n_blk)])
    table = call(functools.partial(odd_near_kernel, negs, tiles), (square,) * 2, (start_e[2], in_vmem(near)))
    vert_o, out = one_pass(1, table[0], vert_o, inner0, *table)
    swap1 = moved(vert_o, 1, -1, True)
    outer1 = moved(out, 1, 2)
    arrays = (vert_o, *map(in_vmem, (near, inner0, *start_e)))
    *table, vert_e = call(functools.partial(even_near_kernel, negs, tiles), (square,) * 4 + (state,), arrays)
    vert_e, out = one_pass(0, table[3], vert_e, outer0, *table[:2])
    swap0 = moved(vert_e, 0, 1, True)
    from_even = moved(far, 0, 1)
    vert_o, out = one_pass(0, vert_e, swap1, out, *table[2:])
    outer2 = moved(out, 0, 3)
    lend = moved(vert_o, 0, 1)
    arrays = (vert_o, in_vmem(far), in_vmem(from_even))
    table = call(functools.partial(odd_far_kernel, negs, tiles), (square,) * 4, arrays)
    coef2, out2 = context_pass(1, table[3], swap0, outer1, *table[:2])
    coef3, out3 = context_pass(1, coef2, lend, out2, *table[2:])
    outer3 = moved(out3, 1, 1)
    arrays = (coef3, *map(in_vmem, (from_even, swap0, outer1, coef2, lend, out2, coef3)))
    *table, vert_e, vert_o = call(functools.partial(last_kernel, negs, tiles), (square, square, state, state), arrays)
    vert_e, out = one_pass(1, table[1], vert_e, outer2, *table)
    back = moved(vert_e, 1, -1)
    vert_done, ctx_done = store(1, (vert_o, out))
    (vert_done,) = store(0, (back,), (vert_done,))
    (ctx_done,) = store(0, (outer3,), (ctx_done,))
    return vert_done, ctx_done


def solution(mesh):
    placed = (
        P(("grp", "blk"), None),
        P(("grp", "blk"), None),
        P(None, ("grp", "blk"), None),
        P(None, None, ("grp", "blk")),
        P(None, ("grp", "blk"), None),
    )

    return jax.shard_map(
        on_device,
        mesh=mesh,
        in_specs=placed,
        out_specs=(P(("grp", "blk"), None), P(("grp", "blk"), None)),
        check_vma=False,
    )
```

```python
import functools
import math

import jax
import jax.numpy as jnp
from jax import lax
from jax.experimental import pallas as pl
from jax.experimental.pallas import tpu as pltpu
from jax.sharding import PartitionSpec as P


F32 = jnp.float32
BF16 = jnp.bfloat16
NT = (((1,), (1,)), ((), ()))
NN = (((1,), (0,)), ((), ()))
CHUNK = 32

VMEM_SPEC = pl.BlockSpec(memory_space=pltpu.VMEM)
HBM_SPEC = pl.BlockSpec(memory_space=pltpu.HBM)
ANY_SPEC = pl.BlockSpec(memory_space=pl.ANY)


def in_vmem(x):
    return pltpu.with_memory_space_constraint(x, pltpu.VMEM)


def in_hbm(x):
    return pltpu.with_memory_space_constraint(x, pltpu.HBM)


def params(mib):
    return pltpu.CompilerParams(vmem_limit_bytes=mib << 20)


def on_core(core):
    return lax.axis_index("blk") % 2 == core


def halves(x):
    high = x.astype(BF16)
    return high, (x - high.astype(F32)).astype(BF16)


def product(a, b, dims):
    along_a, along_b = dims[0][0][0], dims[0][1][0]
    left = jnp.concatenate([a[0], a[0], a[1]], along_a)
    right = jnp.concatenate([b[0], b[1], b[0]], along_b)
    return lax.dot_general(left, right, dims, preferred_element_type=F32)


def row_product(a, b):
    left = jnp.concatenate([a[0], a[0], a[1]], 1)
    right = jnp.concatenate([b[0], b[1], b[0]], 0)
    half = left.shape[0] // 2
    dot = functools.partial(lax.dot_general, dimension_numbers=NN, preferred_element_type=F32)
    return jnp.concatenate([dot(left[:half], right), dot(left[half:], right)], 0)


def negcounts(block_rows, tile, tiles, neg):
    columns = jnp.transpose(neg.astype(F32)).astype(jnp.int32)
    for row in range(0, columns.shape[0], block_rows):
        here = slice(row, row + block_rows)
        picks = [jnp.broadcast_to(columns[here, k : k + 1], (block_rows, tile)) for k in range(neg.shape[0])]
        for tj in range(tiles):
            column = lax.broadcasted_iota(jnp.int32, (block_rows, tile), 1) + tj * tile
            yield here, slice(tj * tile, (tj + 1) * tile), sum((pick == column).astype(F32) for pick in picks)


def gate_of(mask, tile, scale):
    tiles = mask.shape[0]
    mask = mask.astype(F32) * scale
    spread = [[jnp.broadcast_to(mask[i : i + 1, j : j + 1], (tile, tile)) for j in range(tiles)] for i in range(tiles)]
    return jnp.concatenate([jnp.concatenate(row, 1) for row in spread], 0)


def tables(block, neg, mask, base_ref, slope_ref):
    rows, tiles = base_ref.shape[0], mask.shape[0]
    tile = rows // tiles
    scale = 0.125 / math.sqrt(rows)
    for here, there, negcount in negcounts(CHUNK, tile, tiles, neg):
        ti, tj = here.start // tile, there.start // tile
        count = block(here, there).astype(F32)
        gate = jnp.broadcast_to(mask[ti : ti + 1, tj : tj + 1].astype(F32) * scale, (CHUNK, tile))
        base_ref[here, there] = (count - negcount) * gate
        slope_ref[here, there] = (count + negcount) * gate


def packed_rows(rows, negs, tiles, steps):
    return -(-steps * (rows + negs + tiles) // 8) * 8


def pack_parts(pack, index, steps, negs, tiles):
    rows = pack.shape[1]
    at_neg = steps * rows + index * negs
    at_mask = steps * (rows + negs) + index * tiles
    counts = pack.at[index * rows : (index + 1) * rows]
    return counts, pack[at_neg : at_neg + negs], pack[at_mask : at_mask + tiles, :tiles]


def tables_from(pack, index, steps, negs, tiles, base_ref, slope_ref):
    counts, neg, mask = pack_parts(pack, index, steps, negs, tiles)
    tables(lambda here, there: counts[here, there], neg, mask, base_ref, slope_ref)


def fill_pack(pack, first, steps, neg, mask):
    negs, tiles, rows = neg.shape[0], mask.shape[0], pack.shape[1]
    for i in range(steps):
        at_neg = steps * rows + i * negs
        at_mask = steps * (rows + negs) + i * tiles
        pack[at_neg : at_neg + negs] = neg[:, first + i]
        pack[at_mask : at_mask + tiles, :tiles] = mask[:, first + i]


def pass_body(vert, ctx, base, slope):
    vs, cs = halves(vert), halves(ctx)
    coef = base - slope * jnp.tanh(0.5 * product(vs, cs, NT))
    new_ctx = ctx + product(halves(jnp.transpose(coef)), vs, NN)
    new_vert = vert + product(halves(coef), cs, NN)
    return new_vert, new_ctx


def context_part(vs, ctx, coef):
    return ctx + row_product(halves(jnp.transpose(coef)), vs)


def vertex_part(vert, ctx, coef):
    return vert + row_product(halves(coef), halves(ctx))


def first_kernel(core, kept, vert_hbm, ctx_hbm, counts_hbm, neg_hbm, mask_hbm, *refs):
    refs, (cnt, neg, mask, negcount, sems) = refs[:-5], refs[-5:]
    near, far, vert, ctx, coef_ref, new_ctx_ref = refs[kept:]
    rows, tiles = cnt.shape[0], mask.shape[0]
    tile = rows // tiles

    @pl.when(on_core(core))
    def _():
        pairs = [
            (neg_hbm, neg),
            (mask_hbm, mask),
            (vert_hbm, vert),
            (ctx_hbm, ctx),
            (counts_hbm.at[0], cnt),
            (counts_hbm.at[1], near.at[:rows]),
            (counts_hbm.at[2], far.at[:rows]),
            (counts_hbm.at[3], far.at[rows : 2 * rows]),
        ]
        copies = [pltpu.make_async_copy(source, target, sems.at[i]) for i, (source, target) in enumerate(pairs)]
        for copy in copies:
            copy.start()
        copies[0].wait()
        for here, there, value in negcounts(CHUNK, tile, tiles, neg[:, 0]):
            negcount[here, there] = value
        for copy in copies[1:5]:
            copy.wait()
        vs, cs = halves(vert[...]), halves(ctx[...])
        tanh = jnp.tanh(0.5 * product(vs, cs, NT))
        count = cnt[...].astype(F32)
        gate = gate_of(mask[:, 0], tile, 0.125 / math.sqrt(rows))
        coef = gate * ((count - negcount[...]) - (count + negcount[...]) * tanh)
        coef_ref[...] = coef
        new_ctx_ref[...] = context_part(vs, ctx[...], coef)
        fill_pack(near, 1, 1, neg, mask)
        fill_pack(far, 2, 2, neg, mask)
        for copy in copies[5:]:
            copy.wait()


def odd_near_kernel(negs, tiles, after, far_in, near, vert, ctx, coef, far, base_ref, slope_ref, new_vert_ref):
    @pl.when(on_core(1))
    def _():
        tables_from(near, 0, 1, negs, tiles, base_ref, slope_ref)
        new_vert_ref[...] = vertex_part(vert[...], ctx[...], coef[...])


def even_near_kernel(negs, tiles, after, near, mate, vert, ctx, coef, base1, slope1, base2, slope2, new_vert_ref):
    @pl.when(on_core(0))
    def _():
        tables_from(near, 0, 1, negs, tiles, base1, slope1)
        tables_from(mate, 0, 2, negs, tiles, base2, slope2)
        new_vert_ref[...] = vertex_part(vert[...], ctx[...], coef[...])


def odd_far_kernel(negs, tiles, after, own, mate, base2, slope2, own_base3, own_slope3):
    @pl.when(on_core(1))
    def _():
        tables_from(mate, 0, 2, negs, tiles, base2, slope2)
        tables_from(own, 1, 2, negs, tiles, own_base3, own_slope3)


def last_kernel(negs, tiles, after, mate, vert2, ctx2, coef2, vert3, ctx3, coef3, base_ref, slope_ref, even_vert_ref, odd_vert_ref):
    @pl.when(on_core(1))
    def _():
        tables_from(mate, 1, 2, negs, tiles, base_ref, slope_ref)
        even_vert_ref[...] = vertex_part(vert2[...], ctx2[...], coef2[...])
        odd_vert_ref[...] = vertex_part(vert3[...], ctx3[...], coef3[...])


def context_kernel(core, after, vert_ref, ctx_ref, base_ref, slope_ref, coef_ref, new_ctx_ref):
    @pl.when(on_core(core))
    def _():
        vs, cs = halves(vert_ref[...]), halves(ctx_ref[...])
        coef = base_ref[...] - slope_ref[...] * jnp.tanh(0.5 * product(vs, cs, NT))
        coef_ref[...] = coef
        new_ctx_ref[...] = context_part(vs, ctx_ref[...], coef)


def pass_kernel(core, after, vert_ref, ctx_ref, base_ref, slope_ref, new_vert_ref, new_ctx_ref):
    @pl.when(on_core(core))
    def _():
        new_vert_ref[...], new_ctx_ref[...] = pass_body(
            vert_ref[...], ctx_ref[...], base_ref[...], slope_ref[...]
        )


def store_kernel(core, count, *refs):
    sources, targets, sems = refs[:count], refs[-1 - count : -1], refs[-1]

    @pl.when(on_core(core))
    def _():
        copies = [pltpu.make_async_copy(s, t, sems.at[i]) for i, (s, t) in enumerate(zip(sources, targets, strict=True))]
        for copy in copies:
            copy.start()
        for copy in copies:
            copy.wait()


def on_device(vertex_embed, context_embed, counts, negatives, masks):
    part, rows = vertex_embed.shape, counts.shape[1]
    negs, tiles = negatives.shape[1], masks.shape[1]
    vertex_embed, context_embed, counts = in_hbm(vertex_embed), in_hbm(context_embed), in_hbm(counts)
    negatives = in_hbm(jnp.transpose(negatives, (1, 0, 2)))
    masks = in_hbm(jnp.transpose(masks, (1, 0, 2)))
    state = pltpu.VMEM(part, F32)
    square = pltpu.VMEM((rows, rows), F32)
    small = [pltpu.VMEM(negatives.shape, jnp.int32), pltpu.VMEM(masks.shape, jnp.int32)]
    packs = [pltpu.VMEM((packed_rows(rows, negs, tiles, steps), rows), jnp.int32) for steps in (1, 2)]

    def call(kernel, outs, arrays, in_specs=None, **kwargs):
        return pl.pallas_call(
            kernel,
            out_shape=tuple(outs),
            in_specs=in_specs or [ANY_SPEC] + [VMEM_SPEC] * (len(arrays) - 1),
            out_specs=(VMEM_SPEC,) * len(outs),
            compiler_params=params(20),
            **kwargs,
        )(*arrays)

    def first(core, *kept):
        arrays = (vertex_embed, context_embed, counts, negatives, masks, *map(in_vmem, kept))
        return call(
            functools.partial(first_kernel, core, len(kept)),
            (*packs, state, state, square, state),
            arrays,
            [HBM_SPEC] * 5 + [VMEM_SPEC] * len(kept),
            scratch_shapes=[pltpu.VMEM((rows, rows), jnp.int32), *small, square, pltpu.SemaphoreType.DMA((8,))],
            input_output_aliases={5 + i: i for i in range(len(kept))},
        )

    def context_pass(core, after, vert, ctx, base, slope):
        arrays = (after, *map(in_vmem, (vert, ctx, base, slope)))
        return call(functools.partial(context_kernel, core), (square, state), arrays)

    def one_pass(core, after, vert, ctx, base, slope):
        arrays = (after, *map(in_vmem, (vert, ctx, base, slope)))
        return call(functools.partial(pass_kernel, core), (state, state), arrays)

    n_grp, n_blk = lax.axis_size("grp"), lax.axis_size("blk")

    def moved(value, core, blocks, swap=False):
        pairs = [
            (g * n_blk + b, (g ^ swap) * n_blk + (b + blocks) % n_blk) for g in range(n_grp) for b in range(core, n_blk, 2)
        ]
        return lax.ppermute(value, ("grp", "blk"), pairs)

    def store(core, arrays, stored=()):
        count = len(arrays)
        return pl.pallas_call(
            functools.partial(store_kernel, core, count),
            out_shape=(pltpu.HBM(part, F32),) * count,
            in_specs=[VMEM_SPEC] * count + [HBM_SPEC] * len(stored),
            out_specs=(HBM_SPEC,) * count,
            scratch_shapes=[pltpu.SemaphoreType.DMA((count,))],
            input_output_aliases={count + i: i for i in range(len(stored))},
            compiler_params=params(4),
        )(*map(in_vmem, arrays), *stored)

    near, far, *start_o, out = first(1)
    outer0 = moved(out, 1, 1)
    near, far, *start_e, out = first(0, near, far)
    inner0 = moved(out, 0, 1)
    far, *table, vert_o = call(
        functools.partial(odd_near_kernel, negs, tiles),
        (packs[1], square, square, state),
        (start_e[2], *map(in_vmem, (far, near, *start_o))),
        input_output_aliases={1: 0},
    )
    mate = lax.ppermute(far, "blk", [(b, b ^ 1) for b in range(n_blk)])
    vert_o, out = one_pass(1, table[0], vert_o, inner0, *table)
    swap1 = moved(vert_o, 1, -1, True)
    outer1 = moved(out, 1, 2)
    arrays = (vert_o, *map(in_vmem, (near, mate, *start_e)))
    *table, vert_e = call(functools.partial(even_near_kernel, negs, tiles), (square,) * 4 + (state,), arrays)
    vert_e, out = one_pass(0, table[3], vert_e, outer0, *table[:2])
    swap0 = moved(vert_e, 0, 1, True)
    vert_o, out = one_pass(0, vert_e, swap1, out, *table[2:])
    outer2 = moved(out, 0, 3)
    lend = moved(vert_o, 0, 1)
    arrays = (vert_o, in_vmem(far), in_vmem(mate))
    table = call(functools.partial(odd_far_kernel, negs, tiles), (square,) * 4, arrays)
    coef2, out2 = context_pass(1, table[3], swap0, outer1, *table[:2])
    coef3, out3 = context_pass(1, coef2, lend, out2, *table[2:])
    outer3 = moved(out3, 1, 1)
    arrays = (coef3, *map(in_vmem, (mate, swap0, outer1, coef2, lend, out2, coef3)))
    *table, vert_e, vert_o = call(functools.partial(last_kernel, negs, tiles), (square, square, state, state), arrays)
    vert_e, out = one_pass(1, table[1], vert_e, outer2, *table)
    back = moved(vert_e, 1, -1)
    vert_done, ctx_done = store(1, (vert_o, out))
    (vert_done,) = store(0, (back,), (vert_done,))
    (ctx_done,) = store(0, (outer3,), (ctx_done,))
    return vert_done, ctx_done


def solution(mesh):
    placed = (
        P(("grp", "blk"), None),
        P(("grp", "blk"), None),
        P(None, ("grp", "blk"), None),
        P(None, None, ("grp", "blk")),
        P(None, ("grp", "blk"), None),
    )

    return jax.shard_map(
        on_device,
        mesh=mesh,
        in_specs=placed,
        out_specs=(P(("grp", "blk"), None), P(("grp", "blk"), None)),
        check_vma=False,
    )
```

```python
import functools
import math

import jax
import jax.numpy as jnp
from jax import lax
from jax.experimental import pallas as pl
from jax.experimental.pallas import tpu as pltpu
from jax.sharding import PartitionSpec as P


F32 = jnp.float32
BF16 = jnp.bfloat16
NT = (((1,), (1,)), ((), ()))
NN = (((1,), (0,)), ((), ()))
CHUNK = 32

VMEM_SPEC = pl.BlockSpec(memory_space=pltpu.VMEM)
HBM_SPEC = pl.BlockSpec(memory_space=pltpu.HBM)
ANY_SPEC = pl.BlockSpec(memory_space=pl.ANY)


def in_vmem(x):
    return pltpu.with_memory_space_constraint(x, pltpu.VMEM)


def in_hbm(x):
    return pltpu.with_memory_space_constraint(x, pltpu.HBM)


def params(mib):
    return pltpu.CompilerParams(vmem_limit_bytes=mib << 20)


def on_core(core):
    return lax.axis_index("blk") % 2 == core


def halves(x):
    high = x.astype(BF16)
    return high, (x - high.astype(F32)).astype(BF16)


def product(a, b, dims):
    along_a, along_b = dims[0][0][0], dims[0][1][0]
    left = jnp.concatenate([a[0], a[0], a[1]], along_a)
    right = jnp.concatenate([b[0], b[1], b[0]], along_b)
    return lax.dot_general(left, right, dims, preferred_element_type=F32)


def row_product(a, b):
    left = jnp.concatenate([a[0], a[0], a[1]], 1)
    right = jnp.concatenate([b[0], b[1], b[0]], 0)
    half = left.shape[0] // 2
    dot = functools.partial(lax.dot_general, dimension_numbers=NN, preferred_element_type=F32)
    return jnp.concatenate([dot(left[:half], right), dot(left[half:], right)], 0)


def negcounts(block_rows, tile, tiles, neg):
    columns = jnp.transpose(neg.astype(F32)).astype(jnp.int32)
    for row in range(0, columns.shape[0], block_rows):
        here = slice(row, row + block_rows)
        picks = [jnp.broadcast_to(columns[here, k : k + 1], (block_rows, tile)) for k in range(neg.shape[0])]
        for tj in range(tiles):
            column = lax.broadcasted_iota(jnp.int32, (block_rows, tile), 1) + tj * tile
            yield here, slice(tj * tile, (tj + 1) * tile), sum((pick == column).astype(F32) for pick in picks)


def gate_of(mask, tile, scale):
    tiles = mask.shape[0]
    mask = mask.astype(F32) * scale
    spread = [[jnp.broadcast_to(mask[i : i + 1, j : j + 1], (tile, tile)) for j in range(tiles)] for i in range(tiles)]
    return jnp.concatenate([jnp.concatenate(row, 1) for row in spread], 0)


def tables(block, neg, mask, base_ref, slope_ref):
    rows, tiles = base_ref.shape[0], mask.shape[0]
    tile = rows // tiles
    scale = 0.125 / math.sqrt(rows)
    for here, there, negcount in negcounts(CHUNK, tile, tiles, neg):
        ti, tj = here.start // tile, there.start // tile
        count = block(here, there).astype(F32)
        gate = jnp.broadcast_to(mask[ti : ti + 1, tj : tj + 1].astype(F32) * scale, (CHUNK, tile))
        base_ref[here, there] = (count - negcount) * gate
        slope_ref[here, there] = (count + negcount) * gate


def packed_rows(rows, negs, tiles, steps):
    return -(-steps * (rows + negs + tiles) // 8) * 8


def pack_parts(pack, index, steps, negs, tiles):
    rows = pack.shape[1]
    at_neg = steps * rows + index * negs
    at_mask = steps * (rows + negs) + index * tiles
    counts = pack.at[index * rows : (index + 1) * rows]
    return counts, pack[at_neg : at_neg + negs], pack[at_mask : at_mask + tiles, :tiles]


def tables_from(pack, index, steps, negs, tiles, base_ref, slope_ref):
    counts, neg, mask = pack_parts(pack, index, steps, negs, tiles)
    tables(lambda here, there: counts[here, there], neg, mask, base_ref, slope_ref)


def fill_pack(pack, first, steps, neg, mask):
    negs, tiles, rows = neg.shape[0], mask.shape[0], pack.shape[1]
    for i in range(steps):
        at_neg = steps * rows + i * negs
        at_mask = steps * (rows + negs) + i * tiles
        pack[at_neg : at_neg + negs] = neg[:, first + i]
        pack[at_mask : at_mask + tiles, :tiles] = mask[:, first + i]


def pass_body(vert, ctx, base, slope):
    vs, cs = halves(vert), halves(ctx)
    coef = base - slope * jnp.tanh(0.5 * product(vs, cs, NT))
    new_ctx = ctx + product(halves(jnp.transpose(coef)), vs, NN)
    new_vert = vert + product(halves(coef), cs, NN)
    return new_vert, new_ctx


def context_part(vs, ctx, coef):
    return ctx + row_product(halves(jnp.transpose(coef)), vs)


def vertex_part(vert, ctx, coef):
    return vert + row_product(halves(coef), halves(ctx))


def first_kernel(core, kept, vert_hbm, ctx_hbm, counts_hbm, neg_hbm, mask_hbm, *refs):
    refs, (cnt, neg, mask, negcount, sems) = refs[:-5], refs[-5:]
    near, far, vert, ctx, coef_ref, new_ctx_ref = refs[kept:]
    rows, tiles = cnt.shape[0], mask.shape[0]
    tile = rows // tiles

    @pl.when(on_core(core))
    def _():
        pairs = [
            (neg_hbm, neg),
            (mask_hbm, mask),
            (vert_hbm, vert),
            (ctx_hbm, ctx),
            (counts_hbm.at[0], cnt),
            (counts_hbm.at[1], near.at[:rows]),
            (counts_hbm.at[2], far.at[:rows]),
            (counts_hbm.at[3], far.at[rows : 2 * rows]),
        ]
        copies = [pltpu.make_async_copy(source, target, sems.at[i]) for i, (source, target) in enumerate(pairs)]
        for copy in copies:
            copy.start()
        copies[0].wait()
        for here, there, value in negcounts(CHUNK, tile, tiles, neg[:, 0]):
            negcount[here, there] = value
        for copy in copies[1:5]:
            copy.wait()
        vs, cs = halves(vert[...]), halves(ctx[...])
        tanh = jnp.tanh(0.5 * product(vs, cs, NT))
        count = cnt[...].astype(F32)
        gate = gate_of(mask[:, 0], tile, 0.125 / math.sqrt(rows))
        coef = gate * ((count - negcount[...]) - (count + negcount[...]) * tanh)
        coef_ref[...] = coef
        new_ctx_ref[...] = context_part(vs, ctx[...], coef)
        fill_pack(near, 1, 1, neg, mask)
        fill_pack(far, 2, 2, neg, mask)
        for copy in copies[5:]:
            copy.wait()


def odd_near_kernel(negs, tiles, after, near, vert, ctx, coef, base_ref, slope_ref, new_vert_ref):
    @pl.when(on_core(1))
    def _():
        tables_from(near, 0, 1, negs, tiles, base_ref, slope_ref)
        new_vert_ref[...] = vertex_part(vert[...], ctx[...], coef[...])


def even_near_kernel(negs, tiles, after, far_in, near, vert, ctx, coef, far, base_ref, slope_ref, new_vert_ref):
    @pl.when(on_core(0))
    def _():
        tables_from(near, 0, 1, negs, tiles, base_ref, slope_ref)
        new_vert_ref[...] = vertex_part(vert[...], ctx[...], coef[...])


def even_far_kernel(negs, tiles, after, mate, base_ref, slope_ref):
    @pl.when(on_core(0))
    def _():
        tables_from(mate, 0, 2, negs, tiles, base_ref, slope_ref)


def odd_far_kernel(negs, tiles, after, own, mate, base2, slope2, own_base3, own_slope3):
    @pl.when(on_core(1))
    def _():
        tables_from(mate, 0, 2, negs, tiles, base2, slope2)
        tables_from(own, 1, 2, negs, tiles, own_base3, own_slope3)


def last_kernel(negs, tiles, after, mate, vert2, ctx2, coef2, vert3, ctx3, coef3, base_ref, slope_ref, even_vert_ref, odd_vert_ref):
    @pl.when(on_core(1))
    def _():
        tables_from(mate, 1, 2, negs, tiles, base_ref, slope_ref)
        even_vert_ref[...] = vertex_part(vert2[...], ctx2[...], coef2[...])
        odd_vert_ref[...] = vertex_part(vert3[...], ctx3[...], coef3[...])


def context_kernel(core, after, vert_ref, ctx_ref, base_ref, slope_ref, coef_ref, new_ctx_ref):
    @pl.when(on_core(core))
    def _():
        vs, cs = halves(vert_ref[...]), halves(ctx_ref[...])
        coef = base_ref[...] - slope_ref[...] * jnp.tanh(0.5 * product(vs, cs, NT))
        coef_ref[...] = coef
        new_ctx_ref[...] = context_part(vs, ctx_ref[...], coef)


def pass_kernel(core, after, vert_ref, ctx_ref, base_ref, slope_ref, new_vert_ref, new_ctx_ref):
    @pl.when(on_core(core))
    def _():
        new_vert_ref[...], new_ctx_ref[...] = pass_body(
            vert_ref[...], ctx_ref[...], base_ref[...], slope_ref[...]
        )


def store_kernel(core, count, *refs):
    sources, targets, sems = refs[:count], refs[-1 - count : -1], refs[-1]

    @pl.when(on_core(core))
    def _():
        copies = [pltpu.make_async_copy(s, t, sems.at[i]) for i, (s, t) in enumerate(zip(sources, targets, strict=True))]
        for copy in copies:
            copy.start()
        for copy in copies:
            copy.wait()


def on_device(vertex_embed, context_embed, counts, negatives, masks):
    part, rows = vertex_embed.shape, counts.shape[1]
    negs, tiles = negatives.shape[1], masks.shape[1]
    vertex_embed, context_embed, counts = in_hbm(vertex_embed), in_hbm(context_embed), in_hbm(counts)
    negatives = in_hbm(jnp.transpose(negatives, (1, 0, 2)))
    masks = in_hbm(jnp.transpose(masks, (1, 0, 2)))
    state = pltpu.VMEM(part, F32)
    square = pltpu.VMEM((rows, rows), F32)
    small = [pltpu.VMEM(negatives.shape, jnp.int32), pltpu.VMEM(masks.shape, jnp.int32)]
    packs = [pltpu.VMEM((packed_rows(rows, negs, tiles, steps), rows), jnp.int32) for steps in (1, 2)]

    def call(kernel, outs, arrays, in_specs=None, **kwargs):
        return pl.pallas_call(
            kernel,
            out_shape=tuple(outs),
            in_specs=in_specs or [ANY_SPEC] + [VMEM_SPEC] * (len(arrays) - 1),
            out_specs=(VMEM_SPEC,) * len(outs),
            compiler_params=params(20),
            **kwargs,
        )(*arrays)

    def first(core, *kept):
        arrays = (vertex_embed, context_embed, counts, negatives, masks, *map(in_vmem, kept))
        return call(
            functools.partial(first_kernel, core, len(kept)),
            (*packs, state, state, square, state),
            arrays,
            [HBM_SPEC] * 5 + [VMEM_SPEC] * len(kept),
            scratch_shapes=[pltpu.VMEM((rows, rows), jnp.int32), *small, square, pltpu.SemaphoreType.DMA((8,))],
            input_output_aliases={5 + i: i for i in range(len(kept))},
        )

    def context_pass(core, after, vert, ctx, base, slope):
        arrays = (after, *map(in_vmem, (vert, ctx, base, slope)))
        return call(functools.partial(context_kernel, core), (square, state), arrays)

    def one_pass(core, after, vert, ctx, base, slope):
        arrays = (after, *map(in_vmem, (vert, ctx, base, slope)))
        return call(functools.partial(pass_kernel, core), (state, state), arrays)

    n_grp, n_blk = lax.axis_size("grp"), lax.axis_size("blk")

    def moved(value, core, blocks, swap=False):
        pairs = [
            (g * n_blk + b, (g ^ swap) * n_blk + (b + blocks) % n_blk) for g in range(n_grp) for b in range(core, n_blk, 2)
        ]
        return lax.ppermute(value, ("grp", "blk"), pairs)

    def store(core, arrays, stored=()):
        count = len(arrays)
        return pl.pallas_call(
            functools.partial(store_kernel, core, count),
            out_shape=(pltpu.HBM(part, F32),) * count,
            in_specs=[VMEM_SPEC] * count + [HBM_SPEC] * len(stored),
            out_specs=(HBM_SPEC,) * count,
            scratch_shapes=[pltpu.SemaphoreType.DMA((count,))],
            input_output_aliases={count + i: i for i in range(len(stored))},
            compiler_params=params(4),
        )(*map(in_vmem, arrays), *stored)

    near, far, *start_o, out = first(1)
    outer0 = moved(out, 1, 1)
    near, far, *start_e, out = first(0, near, far)
    inner0 = moved(out, 0, 1)
    *table, vert_o = call(
        functools.partial(odd_near_kernel, negs, tiles),
        (square, square, state),
        (start_e[2], *map(in_vmem, (near, *start_o))),
    )
    vert_o, out = one_pass(1, table[0], vert_o, inner0, *table)
    swap1 = moved(vert_o, 1, -1, True)
    outer1 = moved(out, 1, 2)
    far, *table, vert_e = call(
        functools.partial(even_near_kernel, negs, tiles),
        (packs[1], square, square, state),
        (vert_o, *map(in_vmem, (far, near, *start_e))),
        input_output_aliases={1: 0},
    )
    mate = lax.ppermute(far, "blk", [(b, b ^ 1) for b in range(n_blk)])
    vert_e, out = one_pass(0, table[0], vert_e, outer0, *table)
    swap0 = moved(vert_e, 0, 1, True)
    table = call(functools.partial(even_far_kernel, negs, tiles), (square,) * 2, (vert_e, in_vmem(mate)))
    vert_o, out = one_pass(0, table[0], swap1, out, *table)
    outer2 = moved(out, 0, 3)
    lend = moved(vert_o, 0, 1)
    arrays = (vert_o, in_vmem(far), in_vmem(mate))
    table = call(functools.partial(odd_far_kernel, negs, tiles), (square,) * 4, arrays)
    coef2, out2 = context_pass(1, table[3], swap0, outer1, *table[:2])
    coef3, out3 = context_pass(1, coef2, lend, out2, *table[2:])
    outer3 = moved(out3, 1, 1)
    arrays = (coef3, *map(in_vmem, (mate, swap0, outer1, coef2, lend, out2, coef3)))
    *table, vert_e, vert_o = call(functools.partial(last_kernel, negs, tiles), (square, square, state, state), arrays)
    vert_e, out = one_pass(1, table[1], vert_e, outer2, *table)
    back = moved(vert_e, 1, -1)
    vert_done, ctx_done = store(1, (vert_o, out))
    (vert_done,) = store(0, (back,), (vert_done,))
    (ctx_done,) = store(0, (outer3,), (ctx_done,))
    return vert_done, ctx_done


def solution(mesh):
    placed = (
        P(("grp", "blk"), None),
        P(("grp", "blk"), None),
        P(None, ("grp", "blk"), None),
        P(None, None, ("grp", "blk")),
        P(None, ("grp", "blk"), None),
    )

    return jax.shard_map(
        on_device,
        mesh=mesh,
        in_specs=placed,
        out_specs=(P(("grp", "blk"), None), P(("grp", "blk"), None)),
        check_vma=False,
    )
```

```python
import functools
import math

import jax
import jax.numpy as jnp
from jax import lax
from jax.experimental import pallas as pl
from jax.experimental.pallas import tpu as pltpu
from jax.sharding import PartitionSpec as P


F32 = jnp.float32
BF16 = jnp.bfloat16
NT = (((1,), (1,)), ((), ()))
NN = (((1,), (0,)), ((), ()))
CHUNK = 32

VMEM_SPEC = pl.BlockSpec(memory_space=pltpu.VMEM)
HBM_SPEC = pl.BlockSpec(memory_space=pltpu.HBM)
ANY_SPEC = pl.BlockSpec(memory_space=pl.ANY)


def in_vmem(x):
    return pltpu.with_memory_space_constraint(x, pltpu.VMEM)


def in_hbm(x):
    return pltpu.with_memory_space_constraint(x, pltpu.HBM)


def params(mib):
    return pltpu.CompilerParams(vmem_limit_bytes=mib << 20)


def on_core(core):
    return lax.axis_index("blk") % 2 == core


def halves(x):
    high = x.astype(BF16)
    return high, (x - high.astype(F32)).astype(BF16)


def product(a, b, dims):
    along_a, along_b = dims[0][0][0], dims[0][1][0]
    left = jnp.concatenate([a[0], a[0], a[1]], along_a)
    right = jnp.concatenate([b[0], b[1], b[0]], along_b)
    return lax.dot_general(left, right, dims, preferred_element_type=F32)


def row_product(a, b):
    left = jnp.concatenate([a[0], a[0], a[1]], 1)
    right = jnp.concatenate([b[0], b[1], b[0]], 0)
    half = left.shape[0] // 2
    dot = functools.partial(lax.dot_general, dimension_numbers=NN, preferred_element_type=F32)
    return jnp.concatenate([dot(left[:half], right), dot(left[half:], right)], 0)


def negcounts(block_rows, tile, tiles, neg):
    columns = jnp.transpose(neg.astype(F32)).astype(jnp.int32)
    for row in range(0, columns.shape[0], block_rows):
        here = slice(row, row + block_rows)
        picks = [jnp.broadcast_to(columns[here, k : k + 1], (block_rows, tile)) for k in range(neg.shape[0])]
        for tj in range(tiles):
            column = lax.broadcasted_iota(jnp.int32, (block_rows, tile), 1) + tj * tile
            yield here, slice(tj * tile, (tj + 1) * tile), sum((pick == column).astype(F32) for pick in picks)


def gate_of(mask, tile, scale):
    tiles = mask.shape[0]
    mask = mask.astype(F32) * scale
    spread = [[jnp.broadcast_to(mask[i : i + 1, j : j + 1], (tile, tile)) for j in range(tiles)] for i in range(tiles)]
    return jnp.concatenate([jnp.concatenate(row, 1) for row in spread], 0)


def tables(block, neg, mask, base_ref, slope_ref):
    rows, tiles = base_ref.shape[0], mask.shape[0]
    tile = rows // tiles
    scale = 0.125 / math.sqrt(rows)
    for here, there, negcount in negcounts(CHUNK, tile, tiles, neg):
        ti, tj = here.start // tile, there.start // tile
        count = block(here, there).astype(F32)
        gate = jnp.broadcast_to(mask[ti : ti + 1, tj : tj + 1].astype(F32) * scale, (CHUNK, tile))
        base_ref[here, there] = (count - negcount) * gate
        slope_ref[here, there] = (count + negcount) * gate


def packed_rows(rows, negs, tiles, steps):
    return -(-steps * (rows + negs + tiles) // 8) * 8


def pack_parts(pack, index, steps, negs, tiles):
    rows = pack.shape[1]
    at_neg = steps * rows + index * negs
    at_mask = steps * (rows + negs) + index * tiles
    counts = pack.at[index * rows : (index + 1) * rows]
    return counts, pack[at_neg : at_neg + negs], pack[at_mask : at_mask + tiles, :tiles]


def tables_from(pack, index, steps, negs, tiles, base_ref, slope_ref):
    counts, neg, mask = pack_parts(pack, index, steps, negs, tiles)
    tables(lambda here, there: counts[here, there], neg, mask, base_ref, slope_ref)


def fill_pack(pack, first, steps, neg, mask):
    negs, tiles, rows = neg.shape[0], mask.shape[0], pack.shape[1]
    for i in range(steps):
        at_neg = steps * rows + i * negs
        at_mask = steps * (rows + negs) + i * tiles
        pack[at_neg : at_neg + negs] = neg[:, first + i]
        pack[at_mask : at_mask + tiles, :tiles] = mask[:, first + i]


def pass_body(vert, ctx, base, slope):
    vs, cs = halves(vert), halves(ctx)
    coef = base - slope * jnp.tanh(0.5 * product(vs, cs, NT))
    new_ctx = ctx + product(halves(jnp.transpose(coef)), vs, NN)
    new_vert = vert + product(halves(coef), cs, NN)
    return new_vert, new_ctx


def context_part(vs, ctx, coef):
    return ctx + row_product(halves(jnp.transpose(coef)), vs)


def vertex_part(vert, ctx, coef):
    return vert + row_product(halves(coef), halves(ctx))


def first_kernel(core, kept, vert_hbm, ctx_hbm, counts_hbm, neg_hbm, mask_hbm, *refs):
    refs, (cnt, neg, mask, negcount, sems) = refs[:-5], refs[-5:]
    near, far, vert, ctx, coef_ref, new_ctx_ref = refs[kept:]
    rows, tiles = cnt.shape[0], mask.shape[0]
    tile = rows // tiles

    @pl.when(on_core(core))
    def _():
        pairs = [
            (neg_hbm, neg),
            (mask_hbm, mask),
            (vert_hbm, vert),
            (ctx_hbm, ctx),
            (counts_hbm.at[0], cnt),
            (counts_hbm.at[1], near.at[:rows]),
            (counts_hbm.at[2], far.at[:rows]),
            (counts_hbm.at[3], far.at[rows : 2 * rows]),
        ]
        copies = [pltpu.make_async_copy(source, target, sems.at[i]) for i, (source, target) in enumerate(pairs)]
        for copy in copies:
            copy.start()
        copies[0].wait()
        for here, there, value in negcounts(CHUNK, tile, tiles, neg[:, 0]):
            negcount[here, there] = value
        for copy in copies[1:5]:
            copy.wait()
        vs, cs = halves(vert[...]), halves(ctx[...])
        tanh = jnp.tanh(0.5 * product(vs, cs, NT))
        count = cnt[...].astype(F32)
        gate = gate_of(mask[:, 0], tile, 0.125 / math.sqrt(rows))
        coef = gate * ((count - negcount[...]) - (count + negcount[...]) * tanh)
        coef_ref[...] = coef
        new_ctx_ref[...] = context_part(vs, ctx[...], coef)
        fill_pack(near, 1, 1, neg, mask)
        fill_pack(far, 2, 2, neg, mask)
        for copy in copies[5:]:
            copy.wait()


def odd_near_kernel(negs, tiles, after, near, vert, ctx, coef, base_ref, slope_ref, new_vert_ref):
    @pl.when(on_core(1))
    def _():
        tables_from(near, 0, 1, negs, tiles, base_ref, slope_ref)
        new_vert_ref[...] = vertex_part(vert[...], ctx[...], coef[...])


def even_near_kernel(negs, tiles, after, far_in, near, vert, ctx, coef, far, base_ref, slope_ref, new_vert_ref):
    @pl.when(on_core(0))
    def _():
        tables_from(near, 0, 1, negs, tiles, base_ref, slope_ref)
        new_vert_ref[...] = vertex_part(vert[...], ctx[...], coef[...])


def even_far_kernel(negs, tiles, after, mate, base_ref, slope_ref):
    @pl.when(on_core(0))
    def _():
        tables_from(mate, 0, 2, negs, tiles, base_ref, slope_ref)


def odd_far_kernel(negs, tiles, after, own, mate, base2, slope2, own_base3, own_slope3, base, slope):
    @pl.when(on_core(1))
    def _():
        for pack, index, base_ref, slope_ref in ((mate, 0, base2, slope2), (own, 1, own_base3, own_slope3)):
            tables_from(pack, index, 2, negs, tiles, base, slope)
            base_ref[...] = jnp.transpose(base[...])
            slope_ref[...] = jnp.transpose(slope[...])


def last_kernel(negs, tiles, after, mate, vert2, ctx2, coef2, vert3, ctx3, coef3, base_ref, slope_ref, even_vert_ref, odd_vert_ref):
    @pl.when(on_core(1))
    def _():
        tables_from(mate, 1, 2, negs, tiles, base_ref, slope_ref)
        even_vert_ref[...] = vertex_part(vert2[...], ctx2[...], jnp.transpose(coef2[...]))
        odd_vert_ref[...] = vertex_part(vert3[...], ctx3[...], jnp.transpose(coef3[...]))


def context_kernel(core, after, vert_ref, ctx_ref, base_ref, slope_ref, coef_ref, new_ctx_ref):
    @pl.when(on_core(core))
    def _():
        vs, cs = halves(vert_ref[...]), halves(ctx_ref[...])
        coef = base_ref[...] - slope_ref[...] * jnp.tanh(0.5 * product(cs, vs, NT))
        coef_ref[...] = coef
        new_ctx_ref[...] = ctx_ref[...] + row_product(halves(coef), vs)


def pass_kernel(core, after, vert_ref, ctx_ref, base_ref, slope_ref, new_vert_ref, new_ctx_ref):
    @pl.when(on_core(core))
    def _():
        new_vert_ref[...], new_ctx_ref[...] = pass_body(
            vert_ref[...], ctx_ref[...], base_ref[...], slope_ref[...]
        )


def store_kernel(core, count, *refs):
    sources, targets, sems = refs[:count], refs[-1 - count : -1], refs[-1]

    @pl.when(on_core(core))
    def _():
        copies = [pltpu.make_async_copy(s, t, sems.at[i]) for i, (s, t) in enumerate(zip(sources, targets, strict=True))]
        for copy in copies:
            copy.start()
        for copy in copies:
            copy.wait()


def on_device(vertex_embed, context_embed, counts, negatives, masks):
    part, rows = vertex_embed.shape, counts.shape[1]
    negs, tiles = negatives.shape[1], masks.shape[1]
    vertex_embed, context_embed, counts = in_hbm(vertex_embed), in_hbm(context_embed), in_hbm(counts)
    negatives = in_hbm(jnp.transpose(negatives, (1, 0, 2)))
    masks = in_hbm(jnp.transpose(masks, (1, 0, 2)))
    state = pltpu.VMEM(part, F32)
    square = pltpu.VMEM((rows, rows), F32)
    small = [pltpu.VMEM(negatives.shape, jnp.int32), pltpu.VMEM(masks.shape, jnp.int32)]
    packs = [pltpu.VMEM((packed_rows(rows, negs, tiles, steps), rows), jnp.int32) for steps in (1, 2)]

    def call(kernel, outs, arrays, in_specs=None, **kwargs):
        return pl.pallas_call(
            kernel,
            out_shape=tuple(outs),
            in_specs=in_specs or [ANY_SPEC] + [VMEM_SPEC] * (len(arrays) - 1),
            out_specs=(VMEM_SPEC,) * len(outs),
            compiler_params=params(20),
            **kwargs,
        )(*arrays)

    def first(core, *kept):
        arrays = (vertex_embed, context_embed, counts, negatives, masks, *map(in_vmem, kept))
        return call(
            functools.partial(first_kernel, core, len(kept)),
            (*packs, state, state, square, state),
            arrays,
            [HBM_SPEC] * 5 + [VMEM_SPEC] * len(kept),
            scratch_shapes=[pltpu.VMEM((rows, rows), jnp.int32), *small, square, pltpu.SemaphoreType.DMA((8,))],
            input_output_aliases={5 + i: i for i in range(len(kept))},
        )

    def context_pass(core, after, vert, ctx, base, slope):
        arrays = (after, *map(in_vmem, (vert, ctx, base, slope)))
        return call(functools.partial(context_kernel, core), (square, state), arrays)

    def one_pass(core, after, vert, ctx, base, slope):
        arrays = (after, *map(in_vmem, (vert, ctx, base, slope)))
        return call(functools.partial(pass_kernel, core), (state, state), arrays)

    n_grp, n_blk = lax.axis_size("grp"), lax.axis_size("blk")

    def moved(value, core, blocks, swap=False):
        pairs = [
            (g * n_blk + b, (g ^ swap) * n_blk + (b + blocks) % n_blk) for g in range(n_grp) for b in range(core, n_blk, 2)
        ]
        return lax.ppermute(value, ("grp", "blk"), pairs)

    def store(core, arrays, stored=()):
        count = len(arrays)
        return pl.pallas_call(
            functools.partial(store_kernel, core, count),
            out_shape=(pltpu.HBM(part, F32),) * count,
            in_specs=[VMEM_SPEC] * count + [HBM_SPEC] * len(stored),
            out_specs=(HBM_SPEC,) * count,
            scratch_shapes=[pltpu.SemaphoreType.DMA((count,))],
            input_output_aliases={count + i: i for i in range(len(stored))},
            compiler_params=params(4),
        )(*map(in_vmem, arrays), *stored)

    near, far, *start_o, out = first(1)
    outer0 = moved(out, 1, 1)
    near, far, *start_e, out = first(0, near, far)
    inner0 = moved(out, 0, 1)
    *table, vert_o = call(
        functools.partial(odd_near_kernel, negs, tiles),
        (square, square, state),
        (start_e[2], *map(in_vmem, (near, *start_o))),
    )
    vert_o, out = one_pass(1, table[0], vert_o, inner0, *table)
    swap1 = moved(vert_o, 1, -1, True)
    outer1 = moved(out, 1, 2)
    far, *table, vert_e = call(
        functools.partial(even_near_kernel, negs, tiles),
        (packs[1], square, square, state),
        (vert_o, *map(in_vmem, (far, near, *start_e))),
        input_output_aliases={1: 0},
    )
    mate = lax.ppermute(far, "blk", [(b, b ^ 1) for b in range(n_blk)])
    vert_e, out = one_pass(0, table[0], vert_e, outer0, *table)
    swap0 = moved(vert_e, 0, 1, True)
    table = call(functools.partial(even_far_kernel, negs, tiles), (square,) * 2, (vert_e, in_vmem(mate)))
    vert_o, out = one_pass(0, table[0], swap1, out, *table)
    outer2 = moved(out, 0, 3)
    lend = moved(vert_o, 0, 1)
    arrays = (vert_o, in_vmem(far), in_vmem(mate))
    table = call(functools.partial(odd_far_kernel, negs, tiles), (square,) * 4, arrays, scratch_shapes=[square, square])
    coef2, out2 = context_pass(1, table[3], swap0, outer1, *table[:2])
    coef3, out3 = context_pass(1, coef2, lend, out2, *table[2:])
    outer3 = moved(out3, 1, 1)
    arrays = (coef3, *map(in_vmem, (mate, swap0, outer1, coef2, lend, out2, coef3)))
    *table, vert_e, vert_o = call(functools.partial(last_kernel, negs, tiles), (square, square, state, state), arrays)
    vert_e, out = one_pass(1, table[1], vert_e, outer2, *table)
    back = moved(vert_e, 1, -1)
    vert_done, ctx_done = store(1, (vert_o, out))
    (vert_done,) = store(0, (back,), (vert_done,))
    (ctx_done,) = store(0, (outer3,), (ctx_done,))
    return vert_done, ctx_done


def solution(mesh):
    placed = (
        P(("grp", "blk"), None),
        P(("grp", "blk"), None),
        P(None, ("grp", "blk"), None),
        P(None, None, ("grp", "blk")),
        P(None, ("grp", "blk"), None),
    )

    return jax.shard_map(
        on_device,
        mesh=mesh,
        in_specs=placed,
        out_specs=(P(("grp", "blk"), None), P(("grp", "blk"), None)),
        check_vma=False,
    )
```
